128 devices in a mesh: slide: 16 (over z, y_hi, core), tile: 8 (over y_lo, x).
Axes of the slice: x: 4, y: 4 (y_hi: 2, y_lo: 2; y = y_hi * 2 + y_lo), z: 4, core: 2. Of those that a mesh axis runs over, the one named last changes fastest.
Arguments:
- features: bfloat16 [16, 8, 32, 32, 768], P('slide', 'tile'), may hold values from -6 to 6
- cotangent: bfloat16 [16, 8, 32, 32, 768], P('slide', 'tile'), may hold values from -0.59765625 to 0.59765625
- neighbours: int32 [16, 8, 8], P('slide'), may hold values from 0 to 8, as said below
- skip_flags: int32 [1, 16], P(None, 'slide'), may hold values 0 or 1
- dw_weight: float32 [1, 7, 7, 768], replicated, may hold values from -0.875 to 0.875
- ln_gain: float32 [1, 768], replicated, may hold values from 0.5 to 1.5
- ln_bias: float32 [1, 768], replicated, may hold values from -3 to 3
- up_weight: bfloat16 [1, 3072, 768], replicated, may hold values from -0.21875 to 0.21875
- up_bias: float32 [1, 3072], replicated, may hold values from -3 to 3
- down_weight: bfloat16 [1, 768, 3072], replicated, may hold values from -0.109375 to 0.109375
- down_bias: float32 [1, 768], replicated, may hold values from -3 to 3
- layer_scale: float32 [1, 768], replicated, may hold values from 0.5 to 1.5
Outputs:
- block_out: bfloat16 [16, 8, 32, 32, 768], P('slide', 'tile')
- input_grad: bfloat16 [16, 8, 32, 32, 768], P('slide', 'tile')
- weight_grads: float32 [1, 3072, 1536], P(None, ('slide', 'tile'))
- kernel_grads: float32 [1, 7, 7, 768], replicated
- channel_grads: float32 [1, 4, 768], replicated
- bias_grads: float32 [1, 3072], replicated
The draws below stay inside these ranges and needn't reach their ends.
Inputs may be any that keep to these rules, and one draw needn't show every extreme that they name: neighbours[s, a, d] is the tile of slide s next to tile a in direction d, or 8 where no tissue tile lies there; tiles of a slide sit on a grid four tiles wide, and b is a's neighbour in one direction exactly when a is b's in the opposite direction.
All inputs are finite; a program needn't handle non-finite values. No bound on the sum of `skip_flags` on one device may be relied on, other than what follows from the above.
Results may differ from the reference program's by a relative error of at most 0.015.
Values may be sent and summed in bfloat16 or wider, within the bound.
No kernel may reach another device: no remote copies, remote signals or barrier semaphores. Data moves between devices by JAX's collectives and lax.ppermute only.
A program may use at most 192 MiB of HBM per device.

```python
import jax
import jax.numpy as jnp
from jax import lax

C = 768
HID = 3072
SIDE = 32
BLOCKS = 1
TILES = 8
SLIDES = 16


def draw_neighbours(key, part):
    step_rows = jnp.array([-1, 1, 0, 0, -1, -1, 1, 1], jnp.int32)
    step_columns = jnp.array([0, 0, -1, 1, -1, 1, -1, 1], jnp.int32)
    positions = jnp.arange(TILES, dtype=jnp.int32)

    def one_slide(slide_key):
        cells = jax.random.permutation(slide_key, 2 * TILES)[:TILES].astype(jnp.int32)
        grid_row = cells // 4
        grid_column = cells % 4
        wanted_row = grid_row[:, None] + step_rows[None, :]
        wanted_column = grid_column[:, None] + step_columns[None, :]
        matches = ((grid_row[None, None, :] == wanted_row[:, :, None]) & (grid_column[None, None, :] == wanted_column[:, :, None])).astype(jnp.int32)
        found = jnp.sum(matches, axis=2)
        which = jnp.sum(matches * positions[None, None, :], axis=2)
        return jnp.where(found > 0, which, TILES).astype(jnp.int32)
    slide_keys = jax.random.split(jax.random.fold_in(key, 7), SLIDES)
    return jax.vmap(one_slide)(slide_keys)


def place_ends(result, own_key, low, top_value):
    longest = result.shape.index(max(result.shape))
    spots = []
    for shift in (0, 1):
        where = [jax.random.randint(jax.random.fold_in(own_key, axis), (), 0, length) for axis, length in enumerate(result.shape)]
        where[longest] = (where[longest] + shift) % result.shape[longest]
        spots.append(tuple(where))
    return result.at[spots[0]].set(low).at[spots[1]].set(top_value)


def block_scale(stream_key, shape, pieces, least, top_value):
    level = 1.0
    for axis_at, blocks in pieces:
        steps = jax.random.uniform(jax.random.fold_in(jax.random.fold_in(stream_key, 6), axis_at), (blocks,), jnp.float32, least / len(pieces), top_value / len(pieces))
        level = level * jnp.repeat(jnp.exp(steps), shape[axis_at] // blocks).reshape((-1,) + (1,) * (len(shape) - 1 - axis_at))
    return level


def normal_values(key, shape, width, reach, cuts=(), held_as=jnp.bfloat16):
    values = width * jax.random.normal(key, shape, jnp.float32)
    if cuts:
        values = values * block_scale(key, shape, cuts, -0.22, 0.18)
    return jnp.clip(values, -reach, reach).astype(held_as)


def setup_inputs(seed: int = 0) -> dict:
    seeds = jax.random.split(jax.random.key(seed), 13)
    features = normal_values(seeds[0], (SLIDES, TILES, SIDE, SIDE, C), 1.0, 6.0, ((0, 16), (1, 8)))
    cotangent = normal_values(seeds[1], (SLIDES, TILES, SIDE, SIDE, C), 0.1, 0.59765625, ((0, 16), (1, 8)))
    neighbours = draw_neighbours(jax.random.fold_in(seeds[12], 71), 0)
    skip_flags = place_ends((jax.random.randint(seeds[3], (BLOCKS, SLIDES), 0, 4) < 1).astype(jnp.int32), jax.random.fold_in(seeds[3], 1), 0, 1)
    dw_weight = normal_values(seeds[4], (BLOCKS, 7, 7, C), 49 ** -0.5, 0.875, (), jnp.float32)
    ln_gain = jnp.clip(1.0 + 0.1 * jax.random.normal(seeds[5], (BLOCKS, C), jnp.float32), 0.5, 1.5)
    ln_bias = normal_values(seeds[6], (BLOCKS, C), 0.5, 3.0, (), jnp.float32)
    up_weight = normal_values(seeds[7], (BLOCKS, HID, C), C ** -0.5, 0.21875)
    up_bias = normal_values(seeds[8], (BLOCKS, HID), 0.5, 3.0, (), jnp.float32)
    down_weight = normal_values(seeds[9], (BLOCKS, C, HID), HID ** -0.5, 0.109375)
    down_bias = normal_values(seeds[10], (BLOCKS, C), 0.5, 3.0, (), jnp.float32)
    layer_scale = jnp.clip(jax.random.uniform(seeds[11], (BLOCKS, C), jnp.float32, 0.5, 1.5), 0.5, 1.5)
    return {"features": features, "cotangent": cotangent, "neighbours": neighbours, "skip_flags": skip_flags, "dw_weight": dw_weight, "ln_gain": ln_gain, "ln_bias": ln_bias, "up_weight": up_weight, "up_bias": up_bias, "down_weight": down_weight, "down_bias": down_bias, "layer_scale": layer_scale}


ln_eps = 1e-06
root_half = 0.7071067811865476
inv_root_two_pi = 0.3989422804014327
conv_dims = ('NHWC', 'HWIO', 'NHWC')

def assemble(tiles, table):
    padded = jnp.concatenate([tiles, jnp.zeros_like(tiles[:1])], 0)
    nearby = padded[table]
    upper = jnp.concatenate([nearby[:, 4, -3:, -3:], nearby[:, 0, -3:, :], nearby[:, 5, -3:, :3]], 2)
    middle = jnp.concatenate([nearby[:, 2, :, -3:], tiles, nearby[:, 3, :, :3]], 2)
    lower = jnp.concatenate([nearby[:, 6, :3, -3:], nearby[:, 1, :3, :], nearby[:, 7, :3, :3]], 2)
    return jnp.concatenate([upper, middle, lower], 1)

def depthwise(extended, kernel):
    channels = kernel.shape[-1]
    return lax.conv_general_dilated(extended, kernel[:, :, None, :], (1, 1), 'VALID', dimension_numbers=conv_dims, feature_group_count=channels, precision=lax.Precision.HIGHEST)

def kernel_grad(extended, conv_grad):
    channels = conv_grad.shape[-1]
    total = jnp.zeros((7, 7, channels), jnp.float32)
    for tile_pos in range(conv_grad.shape[0]):
        kernel = jnp.transpose(conv_grad[tile_pos:tile_pos + 1], (1, 2, 0, 3))
        single = lax.conv_general_dilated(extended[tile_pos:tile_pos + 1], kernel, (1, 1), 'VALID', dimension_numbers=conv_dims, feature_group_count=channels, precision=lax.Precision.HIGHEST)
        total = total + single[0]
    return total

def normalize(values):
    average = lax.optimization_barrier(jnp.mean(values, axis=-1, keepdims=True))
    centred = values - average
    inv_std = lax.rsqrt(lax.optimization_barrier(jnp.mean(centred * centred, axis=-1, keepdims=True)) + ln_eps)
    return (centred * inv_std, inv_std)

def gelu_parts(pre):
    cdf = 0.5 * (1.0 + lax.erf(pre * root_half))
    return (cdf, cdf + pre * inv_root_two_pi * jnp.exp(-0.5 * pre * pre))

def contract(left, right):
    return lax.dot_general(left, right, (((1,), (1,)), ((), ())), preferred_element_type=jnp.float32)

def over_pixels(left, right):
    return lax.dot_general(left, right, (((0,), (0,)), ((), ())), preferred_element_type=jnp.float32)

def reference(features, cotangent, neighbours, skip_flags, dw_weight, ln_gain, ln_bias, up_weight, up_bias, down_weight, down_bias, layer_scale):
    blocks = dw_weight.shape[0]
    channels = features.shape[-1]
    hidden_units = up_weight.shape[1]
    tile_shape = features.shape[1:]

    def one_slide(totals, slide_data):
        tiles, tile_grad, table, skips = slide_data
        current = tiles
        saved = []
        for layer in range(blocks):
            keep = (1 - skips[layer]).astype(jnp.float32)
            extended = assemble(current, table).astype(jnp.float32)
            conv = depthwise(extended, dw_weight[layer])
            whitened, inv_std = normalize(conv.reshape(-1, channels))
            flat = (whitened * ln_gain[layer] + ln_bias[layer]).astype(jnp.bfloat16)
            pre = contract(flat, up_weight[layer]) + up_bias[layer]
            cdf, slope = gelu_parts(pre)
            act = (pre * cdf).astype(jnp.bfloat16)
            branch = contract(act, down_weight[layer]) + down_bias[layer]
            output = (current.astype(jnp.float32).reshape(-1, channels) + keep * layer_scale[layer] * branch).astype(jnp.bfloat16)
            saved.append((extended, whitened, inv_std, flat, pre, act, branch, keep))
            current = output.reshape(tile_shape)
        weight_total, kernel_total, channel_total, bias_total = totals
        step_grad = tile_grad
        for layer in reversed(range(blocks)):
            extended, whitened, inv_std, flat, pre, act, branch, keep = saved[layer]
            grad_flat = step_grad.astype(jnp.float32).reshape(-1, channels)
            scale_grad = lax.optimization_barrier(jnp.sum(grad_flat * keep * branch, axis=0))
            branch_grad = (keep * layer_scale[layer] * grad_flat).astype(jnp.bfloat16)
            act_grad = jnp.dot(branch_grad, down_weight[layer], preferred_element_type=jnp.float32)
            cdf, slope = gelu_parts(pre)
            pre_grad = (act_grad * slope).astype(jnp.bfloat16)
            normed_grad = jnp.dot(pre_grad, up_weight[layer], preferred_element_type=jnp.float32)
            scaled = normed_grad * ln_gain[layer]
            conv_grad = inv_std * (scaled - lax.optimization_barrier(jnp.mean(scaled, axis=-1, keepdims=True)) - whitened * lax.optimization_barrier(jnp.mean(scaled * whitened, axis=-1, keepdims=True)))
            conv_grad = conv_grad.astype(jnp.bfloat16).reshape(tile_shape)
            weight_term = jnp.concatenate([over_pixels(pre_grad, flat), over_pixels(act, branch_grad)], 1)
            weight_total = weight_total.at[layer].add(weight_term)
            kernel_total = kernel_total.at[layer].add(kernel_grad(extended, conv_grad.astype(jnp.float32)))
            channel_term = jnp.stack([lax.optimization_barrier(jnp.sum(normed_grad * whitened, axis=0)), lax.optimization_barrier(jnp.sum(normed_grad, axis=0)), lax.optimization_barrier(jnp.sum(branch_grad.astype(jnp.float32), axis=0)), scale_grad])
            channel_total = channel_total.at[layer].add(channel_term)
            bias_total = bias_total.at[layer].add(lax.optimization_barrier(jnp.sum(pre_grad.astype(jnp.float32), axis=0)))
            grad_extended = assemble(conv_grad, table).astype(jnp.float32)
            back = depthwise(grad_extended, dw_weight[layer][::-1, ::-1])
            step_grad = (step_grad.astype(jnp.float32) + back).astype(jnp.bfloat16)
        return ((weight_total, kernel_total, channel_total, bias_total), (current, step_grad))
    start = (jnp.zeros((blocks, hidden_units, 2 * channels), jnp.float32), jnp.zeros((blocks, 7, 7, channels), jnp.float32), jnp.zeros((blocks, 4, channels), jnp.float32), jnp.zeros((blocks, hidden_units), jnp.float32))
    totals, results = lax.scan(one_slide, start, (features, cotangent, neighbours, jnp.transpose(skip_flags)))
    block_out, input_grad = results
    weight_grads, kernel_grads, channel_grads, bias_grads = totals
    return (block_out, input_grad, weight_grads, kernel_grads, channel_grads, bias_grads)
```

```python
import functools

import jax
import jax.numpy as jnp
from jax import lax
from jax.experimental import pallas as pl
from jax.experimental.pallas import tpu as pltpu
from jax.sharding import PartitionSpec as P

ln_eps = 1e-06
root_half = 0.7071067811865476
inv_root_two_pi = 0.3989422804014327
f32 = jnp.float32
bf16 = jnp.bfloat16
both_axes = ("slide", "tile")
lanes = 128
side = 32
rim = 3
taps = 7
row_block = 16
own_column = 8
wide = 48
vmem_limit = 58 * 1024 * 1024


def swap(value, distance):
    pairs = [(d, d ^ distance) for d in range(lax.axis_size(both_axes))]
    return lax.ppermute(value, both_axes, pairs)


def pack_kernel(table_ref, tile_ref, *refs):
    outs, column_ref, edge_ref = refs[:7], refs[7], refs[8]
    me = lax.axis_index("tile")
    channels = tile_ref.shape[-1]
    for block in range(channels // lanes):
        here = pl.ds(block * lanes, lanes)
        for which, start, first in ((0, 0, 0), (1, 16, 13)):
            column_ref[...] = tile_ref[:, start : start + 16, here].astype(f32).reshape(16 * side, lanes)
            for c in range(rim):
                edge_ref[which, c, :, here] = column_ref[pl.ds(first + c, side, stride=16), :].astype(bf16)
    for k in range(1, 8):
        peer = jnp.bitwise_xor(me, k)

        def faces(*directions):
            hits = [table_ref[0, me, d] == peer for d in directions]
            return functools.reduce(jnp.logical_or, hits)

        out = outs[k - 1]

        @pl.when(faces(0, 4, 5))
        def _():
            out[...] = tile_ref[0:rim]

        @pl.when(faces(1, 6, 7))
        def _():
            out[...] = tile_ref[side - rim : side]

        @pl.when(faces(2))
        def _():
            out[...] = edge_ref[0]

        @pl.when(faces(3))
        def _():
            out[...] = edge_ref[1]


def pack(table, tile):
    channels = tile.shape[-1]
    strip = jax.ShapeDtypeStruct((rim, side, channels), bf16)
    return pl.pallas_call(
        pack_kernel,
        out_shape=[strip] * 7,
        in_specs=[pl.BlockSpec(memory_space=pltpu.SMEM), pl.BlockSpec(memory_space=pltpu.VMEM)],
        out_specs=[pl.BlockSpec(memory_space=pltpu.VMEM)] * 7,
        scratch_shapes=[
            pltpu.VMEM((16 * side, lanes), f32),
            pltpu.VMEM((2, rim, side, channels), bf16),
        ],
        name="pack_strips",
    )(table, tile)


def exchange_strips(table, tile):
    strips = pack(table, tile)
    return [swap(strips[k - 1], k) for k in range(1, 8)]


def assemble(table_ref, tile_ref, strip_refs, stack_ref, extended_ref):
    me = lax.axis_index("tile")
    stack_ref[0] = jnp.zeros((rim, side, lanes), f32)
    for k in range(1, 8):
        stack_ref[k] = strip_refs[k - 1][...].astype(f32)
    extended_ref[rim : rim + side, own_column : own_column + side, :] = tile_ref[...].astype(f32)

    def strip(direction):
        other = table_ref[0, me, direction]
        index = jnp.where(other < 8, jnp.bitwise_xor(other, me), 0)
        return stack_ref[index]

    last = rim + side
    right = own_column + side
    extended_ref[0:rim, own_column:right, :] = strip(0)
    extended_ref[last : last + rim, own_column:right, :] = strip(1)
    west = strip(2)
    east = strip(3)
    for c in range(rim):
        extended_ref[rim:last, own_column - rim + c, :] = west[c]
        extended_ref[rim:last, right + c, :] = east[c]
    extended_ref[0:rim, 0:8, :] = strip(4)[:, side - 8 :]
    extended_ref[0:rim, right : right + 8, :] = strip(5)[:, :8]
    extended_ref[last : last + rim, 0:8, :] = strip(6)[:, side - 8 :]
    extended_ref[last : last + rim, right : right + 8, :] = strip(7)[:, :8]


def spread_weights(weight_ref, spread_ref, flipped):
    for a in range(taps):
        rows = weight_ref[0, taps - 1 - a if flipped else a]
        for b in range(taps):
            at = taps - 1 - b if flipped else b
            spread_ref[b, a] = jnp.broadcast_to(rows[at : at + 1], (8, lanes))


def depthwise(extended_ref, spread_ref, store):
    def rows(block, carry):
        base = block * row_block
        for w in range(side // 8):
            totals = [None] * row_block
            for b in range(taps):
                start = own_column - rim + b + w * 8
                values = [extended_ref[base + r, start : start + 8, :] for r in range(row_block + taps - 1)]
                for a in range(taps):
                    factor = spread_ref[b, a]
                    for r in range(row_block):
                        term = values[r + a] * factor
                        totals[r] = term if totals[r] is None else totals[r] + term
            for r in range(row_block):
                store(base + r, w * 8, totals[r])
        return carry

    lax.fori_loop(0, side // row_block, rows, 0)


def conv_kernel(table_ref, tile_ref, *refs):
    strip_refs, (weight_ref, gain_ref, shift_ref) = refs[:7], refs[7:10]
    whitened_ref, inv_ref, normed_ref, stack_ref, extended_ref, spread_ref, conv_ref = refs[10:]
    block = pl.program_id(0)
    blocks = whitened_ref.shape[1] // lanes
    assemble(table_ref, tile_ref, strip_refs, stack_ref, extended_ref)
    spread_weights(weight_ref, spread_ref, False)

    def store(row, column, value):
        conv_ref[block, row, column : column + 8, :] = value

    depthwise(extended_ref, spread_ref, store)

    @pl.when(block == blocks - 1)
    def _():
        def norm(row, carry):
            parts = [conv_ref[j, row] for j in range(blocks)]
            count = blocks * lanes
            average = jnp.sum(sum(parts), axis=-1, keepdims=True) / count
            centred = [part - average for part in parts]
            spread = jnp.sum(sum(part * part for part in centred), axis=-1, keepdims=True) / count
            inv_std = lax.rsqrt(spread + ln_eps)
            here = pl.ds(pl.multiple_of(row * side, side), side)
            inv_ref[here, :] = inv_std
            for j in range(blocks):
                at = pl.ds(j * lanes, lanes)
                whitened = centred[j] * inv_std
                whitened_ref[here, at] = whitened
                normed_ref[here, at] = (whitened * gain_ref[:, at] + shift_ref[:, at]).astype(bf16)
            return carry

        lax.fori_loop(0, side, norm, 0)


def strip_specs():
    return [pl.BlockSpec((rim, side, lanes), lambda i: (0, 0, i))] * 7


def conv_norm(table, tile, strips, weight, gain, shift):
    channels = tile.shape[-1]
    pixels = side * side
    blocks = channels // lanes
    whole = lambda i: (0, 0)
    return pl.pallas_call(
        conv_kernel,
        grid=(blocks,),
        out_shape=[
            jax.ShapeDtypeStruct((pixels, channels), f32),
            jax.ShapeDtypeStruct((pixels, 1), f32),
            jax.ShapeDtypeStruct((pixels, channels), bf16),
        ],
        in_specs=[
            pl.BlockSpec(memory_space=pltpu.SMEM),
            pl.BlockSpec((side, side, lanes), lambda i: (0, 0, i)),
            *strip_specs(),
            pl.BlockSpec((1, taps, taps, lanes), lambda i: (0, 0, 0, i)),
            pl.BlockSpec((1, channels), whole),
            pl.BlockSpec((1, channels), whole),
        ],
        out_specs=[
            pl.BlockSpec((pixels, channels), whole),
            pl.BlockSpec((pixels, 1), whole),
            pl.BlockSpec((pixels, channels), whole),
        ],
        scratch_shapes=[
            pltpu.VMEM((8, rim, side, lanes), f32),
            pltpu.VMEM((side + 2 * rim, wide, lanes), f32),
            pltpu.VMEM((taps, taps, 8, lanes), f32),
            pltpu.VMEM((blocks, side, side, lanes), f32),
        ],
        compiler_params=pltpu.CompilerParams(vmem_limit_bytes=vmem_limit),
        cost_estimate=pl.CostEstimate(flops=14_000_000_000, bytes_accessed=10_000_000, transcendentals=0),
        name="conv_norm",
    )(table, tile, *strips, weight, gain, shift)


def mlp_kernel(
    skip_ref, normed_ref, grad_ref, tile_ref, whitened_ref, inv_ref, up_ref, up_bias_ref, down_ref,
    down_bias_ref, scale_ref, gain_ref,
    out_ref, conv_grad_ref, mine_ref, theirs_ref, channel_ref, bias_ref,
    branch_grad_ref, branch_ref, normed_grad_ref, act_ref, pre_grad_ref, pair_ref,
):
    step = pl.program_id(0)
    steps = pl.num_programs(0)
    pixels, channels = normed_ref.shape
    keep = (1 - skip_ref[0, 0]).astype(f32)
    factor = keep * scale_ref[...]
    tile_rows = 256

    @pl.when(step == 0)
    def _():
        branch_grad_ref[...] = (factor * grad_ref[...].astype(f32)).astype(bf16)
        branch_ref[...] = jnp.zeros_like(branch_ref)
        normed_grad_ref[...] = jnp.zeros_like(normed_grad_ref)

    dot = functools.partial(lax.dot_general, preferred_element_type=f32)
    by_rows = (((1,), (1,)), ((), ()))
    plain = (((1,), (0,)), ((), ()))
    by_pixels = (((0,), (0,)), ((), ()))
    bias_sum = jnp.zeros((1, up_ref.shape[0]), f32)
    for m in range(pixels // tile_rows):
        rows = pl.ds(m * tile_rows, tile_rows)
        pre = dot(normed_ref[rows, :], up_ref[...], by_rows) + up_bias_ref[...]
        cdf = 0.5 * (1.0 + lax.erf(pre * root_half))
        slope = cdf + pre * inv_root_two_pi * jnp.exp(-0.5 * pre * pre)
        act = (pre * cdf).astype(bf16)
        act_ref[rows, :] = act
        act_grad = dot(branch_grad_ref[rows, :], down_ref[...], plain)
        pre_grad = (act_grad * slope).astype(bf16)
        pre_grad_ref[rows, :] = pre_grad
        bias_sum = bias_sum + jnp.sum(pre_grad.astype(f32), axis=0, keepdims=True)
        branch_ref[rows, :] += dot(act, down_ref[...], by_rows)
        normed_grad_ref[rows, :] += dot(pre_grad, up_ref[...], plain)
    bias_ref[...] = bias_sum
    quarter = pair_ref.shape[1]
    left = dot(pre_grad_ref[...], normed_ref[...], by_pixels).astype(bf16)
    for q in range(4):
        pair_ref[q, :, :channels] = left[q * quarter : (q + 1) * quarter]
    right = dot(act_ref[...], branch_grad_ref[...], by_pixels).astype(bf16)
    for q in range(4):
        pair_ref[q, :, channels:] = right[q * quarter : (q + 1) * quarter]
    core = lax.axis_index("slide") % 2
    for high in range(2):
        mine_ref[0, high] = pair_ref[2 * high + core]
        theirs_ref[0, high] = pair_ref[2 * high + 1 - core]

    @pl.when(step == steps - 1)
    def _():
        rows_each = 64

        def finish(m, sums):
            rows = pl.ds(pl.multiple_of(m * rows_each, rows_each), rows_each)
            grad = grad_ref[rows, :].astype(f32)
            branch = branch_ref[rows, :] + down_bias_ref[...]
            out_ref[rows, :] = (tile_ref[rows, :].astype(f32) + factor * branch).astype(bf16)
            whitened = whitened_ref[rows, :]
            normed_grad = normed_grad_ref[rows, :]
            scaled = normed_grad * gain_ref[...]
            product = normed_grad * whitened
            mean_one = jnp.sum(scaled, axis=-1, keepdims=True) / channels
            mean_two = jnp.sum(scaled * whitened, axis=-1, keepdims=True) / channels
            conv_grad = inv_ref[rows, :] * (scaled - mean_one - whitened * mean_two)
            conv_grad_ref[rows, :] = conv_grad.astype(bf16)
            terms = (product, normed_grad, branch_grad_ref[rows, :].astype(f32), grad * keep * branch)
            return tuple(
                total + jnp.sum(term.reshape(rows_each // 8, 8, channels), axis=0)
                for total, term in zip(sums, terms)
            )

        zero = jnp.zeros((8, channels), f32)
        sums = lax.fori_loop(0, pixels // rows_each, finish, (zero,) * 4)
        for at in range(4):
            channel_ref[at : at + 1, :] = jnp.sum(sums[at], axis=0, keepdims=True)


def mlp(skip, normed, grad, tile, whitened, inv_std, up, up_bias, down, down_bias, scale, gain):
    pixels, channels = normed.shape
    hidden = up.shape[0]
    steps = 4
    chunk = hidden // steps
    quarter = chunk // 4
    once = pl.Buffered(1)
    whole = lambda i: (0, 0)
    full = lambda *shape: pl.BlockSpec(shape, whole, pipeline_mode=once)
    part = jax.ShapeDtypeStruct((steps, 2, quarter, 2 * channels), bf16)
    part_spec = pl.BlockSpec((1, 2, quarter, 2 * channels), lambda i: (i, 0, 0, 0))
    return pl.pallas_call(
        mlp_kernel,
        grid=(steps,),
        out_shape=[
            jax.ShapeDtypeStruct((pixels, channels), bf16),
            jax.ShapeDtypeStruct((pixels, channels), bf16),
            part,
            part,
            jax.ShapeDtypeStruct((4, channels), f32),
            jax.ShapeDtypeStruct((1, hidden), f32),
        ],
        in_specs=[
            pl.BlockSpec(memory_space=pltpu.SMEM),
            full(pixels, channels),
            full(pixels, channels),
            full(pixels, channels),
            full(pixels, channels),
            full(pixels, 1),
            pl.BlockSpec((chunk, channels), lambda i: (i, 0)),
            pl.BlockSpec((1, chunk), lambda i: (0, i)),
            pl.BlockSpec((channels, chunk), lambda i: (0, i)),
            full(1, channels),
            full(1, channels),
            full(1, channels),
        ],
        out_specs=[
            full(pixels, channels),
            full(pixels, channels),
            part_spec,
            part_spec,
            full(4, channels),
            pl.BlockSpec((1, chunk), lambda i: (0, i)),
        ],
        scratch_shapes=[
            pltpu.VMEM((pixels, channels), bf16),
            pltpu.VMEM((pixels, channels), f32),
            pltpu.VMEM((pixels, channels), f32),
            pltpu.VMEM((pixels, chunk), bf16),
            pltpu.VMEM((pixels, chunk), bf16),
            pltpu.VMEM((4, quarter, 2 * channels), bf16),
        ],
        compiler_params=pltpu.CompilerParams(vmem_limit_bytes=vmem_limit),
        cost_estimate=pl.CostEstimate(flops=40_000_000_000, bytes_accessed=40_000_000, transcendentals=0),
        name="mlp_both",
    )(skip, normed, grad, tile, whitened, inv_std, up, up_bias, down, down_bias, scale, gain)


def kernel_grad_kernel(table_ref, tile_ref, *refs):
    strip_refs, grad_ref, out_ref = refs[:7], refs[7], refs[8]
    stack_ref, extended_ref, wide_ref, total_ref = refs[9:]
    assemble(table_ref, tile_ref, strip_refs, stack_ref, extended_ref)
    wide_ref[...] = grad_ref[...].astype(f32)
    total_ref[...] = jnp.zeros_like(total_ref)

    def rows(block, carry):
        base = block * row_block
        for w in range(side // 8):
            grads = [wide_ref[base + r, w * 8 : w * 8 + 8, :] for r in range(row_block)]
            for b in range(taps):
                start = own_column - rim + b + w * 8
                values = [extended_ref[base + r, start : start + 8, :] for r in range(row_block + taps - 1)]
                for a in range(taps):
                    terms = [values[r + a] * grads[r] for r in range(row_block)]
                    while len(terms) > 1:
                        terms = [terms[i] + terms[i + 1] for i in range(0, len(terms), 2)]
                    total_ref[a, b] += terms[0]
        return carry

    lax.fori_loop(0, side // row_block, rows, 0)
    for a in range(taps):
        out_ref[a] = jnp.sum(total_ref[a], axis=1)


def kernel_grad(table, tile, strips, conv_grad):
    channels = tile.shape[-1]
    block_spec = pl.BlockSpec((side, side, lanes), lambda i: (0, 0, i))
    return pl.pallas_call(
        kernel_grad_kernel,
        grid=(channels // lanes,),
        out_shape=jax.ShapeDtypeStruct((taps, taps, channels), f32),
        in_specs=[pl.BlockSpec(memory_space=pltpu.SMEM), block_spec, *strip_specs(), block_spec],
        out_specs=pl.BlockSpec((taps, taps, lanes), lambda i: (0, 0, i)),
        scratch_shapes=[
            pltpu.VMEM((8, rim, side, lanes), f32),
            pltpu.VMEM((side + 2 * rim, wide, lanes), f32),
            pltpu.VMEM((side, side, lanes), f32),
            pltpu.VMEM((taps, taps, 8, lanes), f32),
        ],
        cost_estimate=pl.CostEstimate(flops=14_000_000_000, bytes_accessed=5_000_000, transcendentals=0),
        name="kernel_grad",
    )(table, tile, *strips, conv_grad)


def back_kernel(table_ref, tile_ref, *refs):
    strip_refs, weight_ref, grad_ref, out_ref = refs[:7], refs[7], refs[8], refs[9]
    stack_ref, extended_ref, spread_ref, total_ref = refs[10:]
    assemble(table_ref, tile_ref, strip_refs, stack_ref, extended_ref)
    spread_weights(weight_ref, spread_ref, True)

    def store(row, column, value):
        total_ref[row, column : column + 8, :] = value

    depthwise(extended_ref, spread_ref, store)
    out_ref[...] = (grad_ref[...].astype(f32) + total_ref[...]).astype(bf16)


def back_conv(table, tile, strips, weight, grad):
    channels = tile.shape[-1]
    block_spec = pl.BlockSpec((side, side, lanes), lambda i: (0, 0, i))
    return pl.pallas_call(
        back_kernel,
        grid=(channels // lanes,),
        out_shape=jax.ShapeDtypeStruct(tile.shape, bf16),
        in_specs=[
            pl.BlockSpec(memory_space=pltpu.SMEM),
            block_spec,
            *strip_specs(),
            pl.BlockSpec((1, taps, taps, lanes), lambda i: (0, 0, 0, i)),
            block_spec,
        ],
        out_specs=block_spec,
        scratch_shapes=[
            pltpu.VMEM((8, rim, side, lanes), f32),
            pltpu.VMEM((side + 2 * rim, wide, lanes), f32),
            pltpu.VMEM((taps, taps, 8, lanes), f32),
            pltpu.VMEM((side, side, lanes), f32),
        ],
        cost_estimate=pl.CostEstimate(flops=14_000_000_000, bytes_accessed=5_000_000, transcendentals=0),
        name="back_conv",
    )(table, tile, *strips, weight, grad)


def pick(value, positions):
    for axis, index in positions:
        value = lax.dynamic_index_in_dim(value, index, axis, keepdims=False)
    return value


def fold(parts, dtype):
    wide_parts = [part.astype(f32) for part in parts]
    while len(wide_parts) > 1:
        wide_parts = [wide_parts[i] + wide_parts[i + 1] for i in range(0, len(wide_parts), 2)]
    return wide_parts[0].astype(dtype)


def reduce_axis(take, distance, dtype):
    kept = take(0)
    arrived = [swap(take(k), k * distance) for k in (1, 2, 3)]
    return fold([kept, *arrived], dtype)


def scatter_sum(mine, theirs):
    slide, tile = lax.axis_index("slide"), lax.axis_index("tile")
    z, y_hi = slide // 4, (slide // 2) % 2
    y_lo, x = tile // 4, tile % 4
    steps, _, quarter, width = mine.shape
    rows = quarter // 8

    def take_x(value):
        return lambda k: pick(value, [(value.ndim - 3, x ^ k)])

    def take_y(value):
        return lambda k: pick(value, [(2, y_lo ^ (k % 2)), (1, y_hi ^ (k // 2))])

    def y_stage(value):
        take = take_y(value)
        arrived = [swap(take(k), d) for k, d in ((1, 4), (2, 16), (3, 20))]
        return fold([take(0), *arrived], bf16)

    received = swap(theirs, 8)
    pieces = []
    for piece in range(2):
        here = slice(2 * piece, 2 * piece + 2)
        both = fold([mine[here], received[here]], bf16).reshape(2, 2, 2, 4, rows, width)
        if piece == 0:
            once = reduce_axis(take_x(both), 1, bf16)
            pieces.append(y_stage(once))
        else:
            once = y_stage(both)
            pieces.append(reduce_axis(take_x(once), 1, bf16))
    last = jnp.concatenate(pieces, 0)
    return reduce_axis(lambda k: pick(last, [(0, z ^ k)]), 32, f32)


def sum_everywhere(value):
    value = value + swap(value, 8)
    for distances in ((1, 2, 3), (4, 16, 20), (32, 64, 96)):
        value = fold([value, *[swap(value, d) for d in distances]], f32)
    return value


def on_device(
    features,
    cotangent,
    neighbours,
    skip_flags,
    dw_weight,
    ln_gain,
    ln_bias,
    up_weight,
    up_bias,
    down_weight,
    down_bias,
    layer_scale,
):
    channels = features.shape[-1]
    hidden = up_weight.shape[1]
    tile = features[0, 0]
    grad = cotangent[0, 0]
    flat = (side * side, channels)
    strips = exchange_strips(neighbours, tile)
    whitened, inv_std, normed = conv_norm(neighbours, tile, strips, dw_weight, ln_gain, ln_bias)
    out, conv_grad, mine, theirs, channel_sums, bias_sums = mlp(
        skip_flags, normed, grad.reshape(flat), tile.reshape(flat), whitened, inv_std,
        up_weight[0], up_bias, down_weight[0], down_bias, layer_scale, ln_gain,
    )
    conv_grad = conv_grad.reshape(tile.shape)
    grad_strips = exchange_strips(neighbours, conv_grad)
    weight_rows = scatter_sum(mine, theirs)
    kernel_sums = kernel_grad(neighbours, tile, strips, conv_grad)
    small = jnp.concatenate(
        [kernel_sums.reshape(taps * taps, channels), channel_sums, bias_sums.reshape(-1, channels)], 0
    )
    small = sum_everywhere(small)
    input_grad = back_conv(neighbours, conv_grad, grad_strips, dw_weight, grad)
    split = taps * taps
    return (
        out.reshape(features.shape),
        input_grad[None, None],
        weight_rows[None],
        small[:split].reshape(1, taps, taps, channels),
        small[split : split + 4][None],
        small[split + 4 :].reshape(1, hidden),
    )


def solution(mesh):
    return jax.shard_map(
        on_device,
        mesh=mesh,
        in_specs=(
            P("slide", "tile", None, None, None),
            P("slide", "tile", None, None, None),
            P("slide", None, None),
            P(None, "slide"),
            P(),
            P(),
            P(),
            P(),
            P(),
            P(),
            P(),
            P(),
        ),
        out_specs=(
            P("slide", "tile", None, None, None),
            P("slide", "tile", None, None, None),
            P(None, ("slide", "tile"), None),
            P(),
            P(),
            P(),
        ),
        check_vma=False,
    )
```

```python
import functools

import jax
import jax.numpy as jnp
from jax import lax
from jax.experimental import pallas as pl
from jax.experimental.pallas import tpu as pltpu
from jax.sharding import PartitionSpec as P

ln_eps = 1e-06
root_half = 0.7071067811865476
inv_root_two_pi = 0.3989422804014327
f32 = jnp.float32
bf16 = jnp.bfloat16
both_axes = ("slide", "tile")
lanes = 128
side = 32
rim = 3
taps = 7
row_block = 16
own_column = 8
wide = 48
vmem_limit = 58 * 1024 * 1024


def swap(value, distance):
    pairs = [(d, d ^ distance) for d in range(lax.axis_size(both_axes))]
    return lax.ppermute(value, both_axes, pairs)


def pack_kernel(table_ref, tile_ref, out_ref, column_ref, edge_ref):
    me = lax.axis_index("tile")
    tiles = out_ref.shape[0]
    channels = tile_ref.shape[-1]
    for block in range(channels // lanes):
        here = pl.ds(block * lanes, lanes)
        for which, start, first in ((0, 0, 0), (1, 16, 13)):
            column_ref[...] = tile_ref[:, start : start + 16, here].astype(f32).reshape(16 * side, lanes)
            for c in range(rim):
                edge_ref[which, c, :, here] = column_ref[pl.ds(first + c, side, stride=16), :].astype(bf16)
    sources = (
        lambda: tile_ref[0:rim],
        lambda: tile_ref[side - rim : side],
        lambda: edge_ref[0],
        lambda: edge_ref[1],
    )
    for direction, source in enumerate((0, 1, 2, 3, 0, 0, 1, 1)):
        other = table_ref[0, me, direction]

        @pl.when(other < tiles)
        def _():
            out_ref[other] = sources[source]()


def pack_strips(table, tile):
    tiles = table.shape[1]
    channels = tile.shape[-1]
    return pl.pallas_call(
        pack_kernel,
        out_shape=jax.ShapeDtypeStruct((tiles, rim, side, channels), bf16),
        in_specs=[pl.BlockSpec(memory_space=pltpu.SMEM), pl.BlockSpec(memory_space=pltpu.VMEM)],
        out_specs=pl.BlockSpec(memory_space=pltpu.VMEM),
        scratch_shapes=[
            pltpu.VMEM((16 * side, lanes), f32),
            pltpu.VMEM((2, rim, side, channels), bf16),
        ],
        name="pack_strips",
    )(table, tile)


def assemble(table_ref, tile_ref, strip_ref, extended_ref):
    me = lax.axis_index("tile")
    tiles = strip_ref.shape[0]
    extended_ref[rim : rim + side, own_column : own_column + side, :] = tile_ref[...].astype(f32)

    def strip(direction):
        other = table_ref[0, me, direction]
        values = strip_ref[jnp.minimum(other, tiles - 1)].astype(f32)
        return jnp.where(other < tiles, values, jnp.zeros_like(values))

    last = rim + side
    right = own_column + side
    extended_ref[0:rim, own_column:right, :] = strip(0)
    extended_ref[last : last + rim, own_column:right, :] = strip(1)
    west = strip(2)
    east = strip(3)
    for c in range(rim):
        extended_ref[rim:last, own_column - rim + c, :] = west[c]
        extended_ref[rim:last, right + c, :] = east[c]
    extended_ref[0:rim, 0:8, :] = strip(4)[:, side - 8 :]
    extended_ref[0:rim, right : right + 8, :] = strip(5)[:, :8]
    extended_ref[last : last + rim, 0:8, :] = strip(6)[:, side - 8 :]
    extended_ref[last : last + rim, right : right + 8, :] = strip(7)[:, :8]


def spread_weights(weight_ref, spread_ref, flipped):
    for a in range(taps):
        rows = weight_ref[0, taps - 1 - a if flipped else a]
        for b in range(taps):
            at = taps - 1 - b if flipped else b
            spread_ref[b, a] = jnp.broadcast_to(rows[at : at + 1], (8, lanes))


def depthwise(extended_ref, spread_ref, store):
    def rows(block, carry):
        base = block * row_block
        for w in range(side // 8):
            totals = [None] * row_block
            for b in range(taps):
                start = own_column - rim + b + w * 8
                values = [extended_ref[base + r, start : start + 8, :] for r in range(row_block + taps - 1)]
                for a in range(taps):
                    factor = spread_ref[b, a]
                    for r in range(row_block):
                        term = values[r + a] * factor
                        totals[r] = term if totals[r] is None else totals[r] + term
            for r in range(row_block):
                store(base + r, w * 8, totals[r])
        return carry

    lax.fori_loop(0, side // row_block, rows, 0)


def conv_kernel(table_ref, tile_ref, *refs):
    strip_ref, weight_ref, gain_ref, shift_ref = refs[:4]
    whitened_ref, inv_ref, normed_ref, extended_ref, spread_ref, conv_ref = refs[4:]
    block = pl.program_id(0)
    blocks = whitened_ref.shape[1] // lanes
    assemble(table_ref, tile_ref, strip_ref, extended_ref)
    spread_weights(weight_ref, spread_ref, False)

    def store(row, column, value):
        conv_ref[block, row, column : column + 8, :] = value

    depthwise(extended_ref, spread_ref, store)

    @pl.when(block == blocks - 1)
    def _():
        def norm(row, carry):
            parts = [conv_ref[j, row] for j in range(blocks)]
            count = blocks * lanes
            average = jnp.sum(sum(parts), axis=-1, keepdims=True) / count
            centred = [part - average for part in parts]
            spread = jnp.sum(sum(part * part for part in centred), axis=-1, keepdims=True) / count
            inv_std = lax.rsqrt(spread + ln_eps)
            here = pl.ds(pl.multiple_of(row * side, side), side)
            inv_ref[here, :] = inv_std
            for j in range(blocks):
                at = pl.ds(j * lanes, lanes)
                whitened = centred[j] * inv_std
                whitened_ref[here, at] = whitened
                normed_ref[here, at] = (whitened * gain_ref[:, at] + shift_ref[:, at]).astype(bf16)
            return carry

        lax.fori_loop(0, side, norm, 0)


def strip_spec(strips, first=0):
    return pl.BlockSpec((*strips.shape[:3], lanes), lambda i: (0, 0, 0, first + i))


def conv_norm(table, tile, strips, weight, gain, shift):
    channels = tile.shape[-1]
    pixels = side * side
    blocks = channels // lanes
    whole = lambda i: (0, 0)
    return pl.pallas_call(
        conv_kernel,
        grid=(blocks,),
        out_shape=[
            jax.ShapeDtypeStruct((pixels, channels), f32),
            jax.ShapeDtypeStruct((pixels, 1), f32),
            jax.ShapeDtypeStruct((pixels, channels), bf16),
        ],
        in_specs=[
            pl.BlockSpec(memory_space=pltpu.SMEM),
            pl.BlockSpec((side, side, lanes), lambda i: (0, 0, i)),
            strip_spec(strips),
            pl.BlockSpec((1, taps, taps, lanes), lambda i: (0, 0, 0, i)),
            pl.BlockSpec((1, channels), whole),
            pl.BlockSpec((1, channels), whole),
        ],
        out_specs=[
            pl.BlockSpec((pixels, channels), whole),
            pl.BlockSpec((pixels, 1), whole),
            pl.BlockSpec((pixels, channels), whole),
        ],
        scratch_shapes=[
            pltpu.VMEM((side + 2 * rim, wide, lanes), f32),
            pltpu.VMEM((taps, taps, 8, lanes), f32),
            pltpu.VMEM((blocks, side, side, lanes), f32),
        ],
        compiler_params=pltpu.CompilerParams(vmem_limit_bytes=vmem_limit),
        cost_estimate=pl.CostEstimate(flops=14_000_000_000, bytes_accessed=10_000_000, transcendentals=0),
        name="conv_norm",
    )(table, tile, strips, weight, gain, shift)


dot = functools.partial(lax.dot_general, preferred_element_type=f32)
by_rows = (((1,), (1,)), ((), ()))
plain = (((1,), (0,)), ((), ()))
by_pixels = (((0,), (0,)), ((), ()))


def join_blocks(up_first_ref, up_second_ref, down_first_ref, down_second_ref, up_ref, down_ref):
    block = up_first_ref.shape[0]
    up_ref[:block] = up_first_ref[...]
    up_ref[block:] = up_second_ref[...]
    down_ref[:, :block] = down_first_ref[...]
    down_ref[:, block:] = down_second_ref[...]


def hidden_kernel(
    skip_ref, normed_ref, grad_ref, up_first_ref, up_second_ref, up_bias_ref, down_first_ref, down_second_ref,
    scale_ref,
    act_ref, pre_grad_ref, mine_ref, theirs_ref, bias_ref,
    branch_grad_ref, pair_ref, up_ref, down_ref,
):
    step = pl.program_id(0)
    pixels, channels = normed_ref.shape
    keep = (1 - skip_ref[0, 0]).astype(f32)
    tile_rows = 256
    join_blocks(up_first_ref, up_second_ref, down_first_ref, down_second_ref, up_ref, down_ref)

    @pl.when(step == 0)
    def _():
        branch_grad_ref[...] = (keep * scale_ref[...] * grad_ref[...].astype(f32)).astype(bf16)

    def rows_of(m):
        return pl.ds(m * tile_rows, tile_rows)

    def lift(m):
        return dot(normed_ref[rows_of(m), :], up_ref[...], by_rows) + up_bias_ref[0]

    bias_sum = jnp.zeros((1, up_ref.shape[0]), f32)
    count = pixels // tile_rows
    following = lift(0)
    for m in range(count):
        rows = rows_of(m)
        pre = following
        act_grad = dot(branch_grad_ref[rows, :], down_ref[...], plain)
        if m + 1 < count:
            following = lift(m + 1)
        cdf = 0.5 * (1.0 + lax.erf(pre * root_half))
        slope = cdf + pre * inv_root_two_pi * jnp.exp(-0.5 * pre * pre)
        act_ref[rows, :] = (pre * cdf).astype(bf16)
        pre_grad = (act_grad * slope).astype(bf16)
        pre_grad_ref[rows, :] = pre_grad
        bias_sum = bias_sum + jnp.sum(pre_grad.astype(f32), axis=0, keepdims=True)
    bias_ref[0] = bias_sum
    quarter = pair_ref.shape[1]
    left = dot(pre_grad_ref[...], normed_ref[...], by_pixels).astype(bf16)
    for q in range(4):
        pair_ref[q, :, :channels] = left[q * quarter : (q + 1) * quarter]
    right = dot(act_ref[...], branch_grad_ref[...], by_pixels).astype(bf16)
    for q in range(4):
        pair_ref[q, :, channels:] = right[q * quarter : (q + 1) * quarter]
    core = lax.axis_index("slide") % 2
    for high in range(2):
        mine_ref[0, high] = pair_ref[2 * high + core]
        theirs_ref[0, high] = pair_ref[2 * high + 1 - core]


once = pl.Buffered(1)
anywhere = pl.BlockSpec(memory_space=pl.ANY)
in_scalars = pl.BlockSpec(memory_space=pltpu.SMEM)


def full(*shape):
    return pl.BlockSpec(shape, lambda i: (0, 0), pipeline_mode=once)


def hidden_half(half, skip, normed, grad, up, up_bias, down, scale):
    pixels, channels = normed.shape
    hidden = up.shape[0]
    steps = 2
    chunk = hidden // 4
    quarter = chunk // 4
    block = chunk // 2
    part = jax.ShapeDtypeStruct((steps, 2, quarter, 2 * channels), bf16)
    part_spec = pl.BlockSpec((1, 2, quarter, 2 * channels), lambda i: (i, 0, 0, 0))
    wide_shape = jax.ShapeDtypeStruct((pixels, steps * chunk), bf16)
    wide_spec = pl.BlockSpec((pixels, chunk), lambda i: (0, i))
    return pl.pallas_call(
        hidden_kernel,
        grid=(steps,),
        out_shape=[wide_shape, wide_shape, part, part, jax.ShapeDtypeStruct((steps, 1, chunk), f32)],
        in_specs=[
            in_scalars,
            full(pixels, channels),
            full(pixels, channels),
            pl.BlockSpec((block, channels), lambda i: (4 * i + half, 0)),
            pl.BlockSpec((block, channels), lambda i: (4 * i + 2 + half, 0)),
            pl.BlockSpec((1, 1, chunk), lambda i: (2 * half + i, 0, 0)),
            pl.BlockSpec((channels, block), lambda i: (0, 4 * i + half)),
            pl.BlockSpec((channels, block), lambda i: (0, 4 * i + 2 + half)),
            full(1, channels),
        ],
        out_specs=[wide_spec, wide_spec, part_spec, part_spec, pl.BlockSpec((1, 1, chunk), lambda i: (i, 0, 0))],
        scratch_shapes=[
            pltpu.VMEM((pixels, channels), bf16),
            pltpu.VMEM((4, quarter, 2 * channels), bf16),
            pltpu.VMEM((chunk, channels), bf16),
            pltpu.VMEM((channels, chunk), bf16),
        ],
        compiler_params=pltpu.CompilerParams(vmem_limit_bytes=vmem_limit),
        cost_estimate=pl.CostEstimate(flops=14_000_000_000, bytes_accessed=20_000_000, transcendentals=0),
        name="hidden_half",
    )(skip, normed, grad, up, up, up_bias, down, down, scale)


def join_kernel(
    skip_ref, act_low_ref, act_high_ref, pre_low_ref, pre_high_ref,
    up_first_ref, up_second_ref, down_first_ref, down_second_ref, inv_ref, down_bias_ref, scale_ref, gain_ref, whitened_hbm_ref, tile_hbm_ref, grad_hbm_ref,
    out_ref, conv_grad_ref, channel_ref,
    branch_ref, normed_grad_ref, whitened_ref, tile_ref, grad_ref, arrived, up_ref, down_ref,
):
    step = pl.program_id(0)
    steps = pl.num_programs(0)
    pixels, channels = out_ref.shape
    pairs = ((whitened_hbm_ref, whitened_ref), (tile_hbm_ref, tile_ref), (grad_hbm_ref, grad_ref))
    copies = [pltpu.make_async_copy(*pair, arrived.at[at]) for at, pair in enumerate(pairs)]
    join_blocks(up_first_ref, up_second_ref, down_first_ref, down_second_ref, up_ref, down_ref)

    @pl.when(step == 0)
    def _():
        for copy in copies:
            copy.start()
        branch_ref[...] = dot(act_low_ref[...], down_ref[...], by_rows)
        normed_grad_ref[...] = dot(pre_low_ref[...], up_ref[...], plain)

    @pl.when(step == 1)
    def _():
        branch_ref[...] += dot(act_low_ref[...], down_ref[...], by_rows)
        normed_grad_ref[...] += dot(pre_low_ref[...], up_ref[...], plain)

    @pl.when(step >= 2)
    def _():
        branch_ref[...] += dot(act_high_ref[...], down_ref[...], by_rows)
        normed_grad_ref[...] += dot(pre_high_ref[...], up_ref[...], plain)

    @pl.when(step == steps - 1)
    def _():
        rows_each = 64
        keep = (1 - skip_ref[0, 0]).astype(f32)
        factor = keep * scale_ref[...]
        for copy in copies:
            copy.wait()

        def finish(m, sums):
            rows = pl.ds(pl.multiple_of(m * rows_each, rows_each), rows_each)
            grad = grad_ref[rows, :].astype(f32)
            branch = branch_ref[rows, :] + down_bias_ref[...]
            out_ref[rows, :] = (tile_ref[rows, :].astype(f32) + factor * branch).astype(bf16)
            whitened = whitened_ref[rows, :]
            normed_grad = normed_grad_ref[rows, :]
            scaled = normed_grad * gain_ref[...]
            product = normed_grad * whitened
            mean_one = jnp.sum(scaled, axis=-1, keepdims=True) / channels
            mean_two = jnp.sum(scaled * whitened, axis=-1, keepdims=True) / channels
            conv_grad = inv_ref[rows, :] * (scaled - mean_one - whitened * mean_two)
            conv_grad_ref[rows, :] = conv_grad.astype(bf16)
            branch_grad = (factor * grad).astype(bf16).astype(f32)
            terms = (product, normed_grad, branch_grad, grad * keep * branch)
            return tuple(
                total + jnp.sum(term.reshape(rows_each // 8, 8, channels), axis=0)
                for total, term in zip(sums, terms)
            )

        zero = jnp.zeros((8, channels), f32)
        sums = lax.fori_loop(0, pixels // rows_each, finish, (zero,) * 4)
        for at in range(4):
            channel_ref[at : at + 1, :] = jnp.sum(sums[at], axis=0, keepdims=True)


def join(skip, acts, pre_grads, up, down, inv_std, down_bias, scale, gain, whitened, tile, grad):
    pixels, channels = grad.shape
    chunk = acts[0].shape[1] // 2
    block = chunk // 2
    at_first = lambda i: 4 * (i % 2) + i // 2
    low_spec = pl.BlockSpec((pixels, chunk), lambda i: (0, jnp.minimum(i, 1)))
    high_spec = pl.BlockSpec((pixels, chunk), lambda i: (0, jnp.maximum(i - 2, 0)))
    pixel = jax.ShapeDtypeStruct((pixels, channels), bf16)
    return pl.pallas_call(
        join_kernel,
        grid=(4,),
        out_shape=[pixel, pixel, jax.ShapeDtypeStruct((4, channels), f32)],
        in_specs=[
            in_scalars,
            low_spec,
            high_spec,
            low_spec,
            high_spec,
            pl.BlockSpec((block, channels), lambda i: (at_first(i), 0)),
            pl.BlockSpec((block, channels), lambda i: (at_first(i) + 2, 0)),
            pl.BlockSpec((channels, block), lambda i: (0, at_first(i))),
            pl.BlockSpec((channels, block), lambda i: (0, at_first(i) + 2)),
            full(pixels, 1),
            full(1, channels),
            full(1, channels),
            full(1, channels),
            anywhere,
            anywhere,
            anywhere,
        ],
        out_specs=[full(pixels, channels), full(pixels, channels), full(4, channels)],
        scratch_shapes=[
            pltpu.VMEM((pixels, channels), f32),
            pltpu.VMEM((pixels, channels), f32),
            pltpu.VMEM((pixels, channels), f32),
            pltpu.VMEM((pixels, channels), bf16),
            pltpu.VMEM((pixels, channels), bf16),
            pltpu.SemaphoreType.DMA((3,)),
            pltpu.VMEM((chunk, channels), bf16),
            pltpu.VMEM((channels, chunk), bf16),
        ],
        compiler_params=pltpu.CompilerParams(vmem_limit_bytes=vmem_limit),
        cost_estimate=pl.CostEstimate(flops=14_000_000_000, bytes_accessed=30_000_000, transcendentals=0),
        name="join_halves",
    )(skip, *acts, *pre_grads, up, up, down, down, inv_std, down_bias, scale, gain, whitened, tile, grad)


def kernel_grad_kernel(table_ref, tile_ref, *refs):
    strip_ref, grad_ref, out_ref, extended_ref, wide_ref, total_ref = refs
    assemble(table_ref, tile_ref, strip_ref, extended_ref)
    wide_ref[...] = grad_ref[...].astype(f32)
    total_ref[...] = jnp.zeros_like(total_ref)

    def rows(block, carry):
        base = block * row_block
        for w in range(side // 8):
            grads = [wide_ref[base + r, w * 8 : w * 8 + 8, :] for r in range(row_block)]
            for b in range(taps):
                start = own_column - rim + b + w * 8
                values = [extended_ref[base + r, start : start + 8, :] for r in range(row_block + taps - 1)]
                for a in range(taps):
                    terms = [values[r + a] * grads[r] for r in range(row_block)]
                    while len(terms) > 1:
                        terms = [terms[i] + terms[i + 1] for i in range(0, len(terms), 2)]
                    total_ref[a, b] += terms[0]
        return carry

    lax.fori_loop(0, side // row_block, rows, 0)
    for a in range(taps):
        out_ref[a] = jnp.sum(total_ref[a], axis=1)


def kernel_grad(table, tile, strips, conv_grad):
    channels = tile.shape[-1]
    block_spec = pl.BlockSpec((side, side, lanes), lambda i: (0, 0, i))
    return pl.pallas_call(
        kernel_grad_kernel,
        grid=(channels // lanes,),
        out_shape=jax.ShapeDtypeStruct((taps, taps, channels), f32),
        in_specs=[pl.BlockSpec(memory_space=pltpu.SMEM), block_spec, strip_spec(strips), block_spec],
        out_specs=pl.BlockSpec((taps, taps, lanes), lambda i: (0, 0, i)),
        scratch_shapes=[
            pltpu.VMEM((side + 2 * rim, wide, lanes), f32),
            pltpu.VMEM((side, side, lanes), f32),
            pltpu.VMEM((taps, taps, 8, lanes), f32),
        ],
        cost_estimate=pl.CostEstimate(flops=14_000_000_000, bytes_accessed=5_000_000, transcendentals=0),
        name="kernel_grad",
    )(table, tile, strips, conv_grad)


def back_kernel(table_ref, tile_ref, *refs):
    strip_ref, weight_ref, grad_ref = refs[:3]
    out_ref, extended_ref, spread_ref, total_ref = refs[-4:]
    assemble(table_ref, tile_ref, strip_ref, extended_ref)
    spread_weights(weight_ref, spread_ref, True)

    def store(row, column, value):
        total_ref[row, column : column + 8, :] = value

    depthwise(extended_ref, spread_ref, store)
    out_ref[...] = (grad_ref[...].astype(f32) + total_ref[...]).astype(bf16)


def back_conv(table, tile, strips, weight, grad, part, parts, done=None):
    channels = tile.shape[-1]
    steps = channels // lanes // parts
    first = part * steps
    block_spec = pl.BlockSpec((side, side, lanes), lambda i: (0, 0, first + i))
    earlier = [] if done is None else [done]
    return pl.pallas_call(
        back_kernel,
        grid=(steps,),
        out_shape=jax.ShapeDtypeStruct(tile.shape, bf16),
        in_specs=[
            pl.BlockSpec(memory_space=pltpu.SMEM),
            block_spec,
            strip_spec(strips, first),
            pl.BlockSpec((1, taps, taps, lanes), lambda i: (0, 0, 0, first + i)),
            block_spec,
            *[pl.BlockSpec(memory_space=pl.ANY) for _ in earlier],
        ],
        out_specs=block_spec,
        scratch_shapes=[
            pltpu.VMEM((side + 2 * rim, wide, lanes), f32),
            pltpu.VMEM((taps, taps, 8, lanes), f32),
            pltpu.VMEM((side, side, lanes), f32),
        ],
        input_output_aliases={5: 0} if earlier else {},
        cost_estimate=pl.CostEstimate(
            flops=14_000_000_000 // parts, bytes_accessed=5_000_000 // parts, transcendentals=0
        ),
        name="back_conv",
    )(table, tile, strips, weight, grad, *earlier)


def pick(value, positions):
    for axis, index in positions:
        value = lax.dynamic_index_in_dim(value, index, axis, keepdims=False)
    return value


def fold(parts, dtype):
    wide_parts = [part.astype(f32) for part in parts]
    while len(wide_parts) > 1:
        wide_parts = [wide_parts[i] + wide_parts[i + 1] for i in range(0, len(wide_parts), 2)]
    return wide_parts[0].astype(dtype)


def reduce_axis(take, distance, dtype):
    kept = take(0)
    arrived = [swap(take(k), k * distance) for k in (1, 2, 3)]
    return fold([kept, *arrived], dtype)


def place():
    slide, tile = lax.axis_index("slide"), lax.axis_index("tile")
    return slide // 4, (slide // 2) % 2, tile // 4, tile % 4


def x_parts(value):
    x = place()[3]
    return [pick(value, [(value.ndim - 3, x ^ k)]) for k in range(4)]


def y_parts(value):
    _, y_hi, y_lo, _ = place()
    return [pick(value, [(1, y_lo ^ (k % 2)), (0, y_hi ^ (k // 2))]) for k in range(4)]


def z_parts(value):
    z = place()[0]
    return [pick(value, [(0, z ^ k)]) for k in range(4)]


x_distances = (1, 2, 3)
y_distances = (4, 16, 20)
z_distances = (32, 64, 96)


def gather_sum(parts, distances, dtype):
    arrived = [swap(part, d) for part, d in zip(parts[1:], distances)]
    return fold([parts[0], *arrived], dtype)


def after(value, *others):
    return lax.optimization_barrier((value, *others))[0]


def trade(value, distance, ready):
    arrived = swap(value, distance)
    return after(value, ready) + arrived


def ride(parts, small):
    width = parts[0].shape[-1]
    extra = small.astype(bf16).reshape(-1, width)
    sent = [jnp.concatenate([part.reshape(-1, width), extra], 0) for part in parts[1:]]
    return sent, lax.reduce_precision(small, 8, 7)


def land(sent, small, parts, distances, dtype, ready):
    arrived = [swap(value, d) for value, d in zip(sent, distances)]
    size = parts[0].size // parts[0].shape[-1]
    mine, small = lax.optimization_barrier((parts[0], small, ready))[:2]
    total = fold([mine, *[value[:size].reshape(mine.shape) for value in arrived]], dtype)
    return total, fold([small, *[value[size:].reshape(small.shape) for value in arrived]], f32)


def on_device(
    features,
    cotangent,
    neighbours,
    skip_flags,
    dw_weight,
    ln_gain,
    ln_bias,
    up_weight,
    up_bias,
    down_weight,
    down_bias,
    layer_scale,
):
    channels = features.shape[-1]
    hidden = up_weight.shape[1]
    tile = features[0, 0]
    grad = cotangent[0, 0]
    flat = (side * side, channels)
    strips = lax.all_to_all(pack_strips(neighbours, tile), "tile", 0, 0)
    whitened, inv_std, normed = conv_norm(neighbours, tile, strips, dw_weight, ln_gain, ln_bias)
    flat_grad = grad.reshape(flat)
    bias_order = jnp.swapaxes(up_bias.reshape(4, 2, -1), 0, 1).reshape(4, 1, -1)
    mlp_in = (flat_grad, up_weight[0], bias_order, down_weight[0], layer_scale)
    act_low, pre_low, mine_low, theirs_low, bias_low = hidden_half(0, skip_flags, normed, *mlp_in)
    received_low = swap(theirs_low, 8)
    act_high, pre_high, mine_high, theirs_high, bias_high = hidden_half(1, skip_flags, after(normed, theirs_low), *mlp_in)
    rows = mine_low.shape[2] // 8
    width = mine_low.shape[3]
    grid = (4, 2, 4, rows, width)
    received_high = swap(theirs_high, 8)
    low_x = x_parts(fold([after(mine_low, act_high), received_low], bf16).reshape(grid))
    out, conv_grad, channel_sums = join(
        skip_flags, (after(act_low, *low_x), act_high), (pre_low, pre_high), up_weight[0], down_weight[0],
        inv_std, down_bias, layer_scale, ln_gain, whitened, tile.reshape(flat), flat_grad,
    )
    conv_grad = conv_grad.reshape(tile.shape)
    packed = pack_strips(neighbours, conv_grad)
    low_x[0] = after(low_x[0], packed)
    mine_high = after(mine_high, packed)
    grad_strips = lax.all_to_all(packed, "tile", 0, 0)
    low_z = z_parts(gather_sum(low_x, x_distances, bf16))
    high_z = z_parts(fold([mine_high, received_high], bf16).reshape(grid))
    sent_z = [
        jnp.concatenate([low.reshape(-1, width), high.reshape(-1, width)], 0) for low, high in zip(low_z, high_z)
    ]
    kernel_sums = kernel_grad(neighbours, tile, strips, after(conv_grad, *sent_z))
    small = jnp.concatenate(
        [
            kernel_sums.reshape(taps * taps, channels),
            channel_sums,
            jnp.stack([bias_low.reshape(4, -1), bias_high.reshape(4, -1)], 1).reshape(-1, channels),
        ],
        0,
    )
    count = small.shape[0]
    small = jnp.pad(small, ((0, -count % 16), (0, 0)))
    back = functools.partial(back_conv, neighbours)
    grad_strips = after(grad_strips, small)
    input_grad = back(conv_grad, grad_strips, dw_weight, grad, 0, 3)
    small = trade(small, 8, input_grad)
    input_grad = back(after(conv_grad, small), grad_strips, dw_weight, grad, 1, 3, input_grad)
    small = trade(small, 32, input_grad)
    sent_z[0] = after(sent_z[0], input_grad)
    got_z = gather_sum(sent_z, z_distances, bf16)
    done_low = got_z[: 2 * rows]
    high_x = x_parts(got_z[2 * rows :].reshape(2, 4, rows, width))
    wide_x, small = ride(high_x, small)
    input_grad = back(after(conv_grad, *wide_x), grad_strips, dw_weight, grad, 2, 3, input_grad)
    done_high, small = land(wide_x, small, high_x, x_distances, bf16, input_grad)
    last = y_parts(jnp.concatenate([done_low, done_high.reshape(-1, width)], 0).reshape(2, 2, rows, width))
    wide_y, small = ride(last, small)
    weight_rows, small = land(wide_y, small, last, y_distances, f32, input_grad)
    small = trade(small, 96, small)[:count]
    split = taps * taps
    return (
        out.reshape(features.shape),
        input_grad[None, None],
        weight_rows[None],
        small[:split].reshape(1, taps, taps, channels),
        small[split : split + 4][None],
        small[split + 4 :].reshape(1, hidden),
    )


def solution(mesh):
    return jax.shard_map(
        on_device,
        mesh=mesh,
        in_specs=(
            P("slide", "tile", None, None, None),
            P("slide", "tile", None, None, None),
            P("slide", None, None),
            P(None, "slide"),
            P(),
            P(),
            P(),
            P(),
            P(),
            P(),
            P(),
            P(),
        ),
        out_specs=(
            P("slide", "tile", None, None, None),
            P("slide", "tile", None, None, None),
            P(None, ("slide", "tile"), None),
            P(),
            P(),
            P(),
        ),
        check_vma=False,
    )
```

```python
import functools

import jax
import jax.numpy as jnp
from jax import lax
from jax.experimental import pallas as pl
from jax.experimental.pallas import tpu as pltpu
from jax.sharding import PartitionSpec as P

ln_eps = 1e-06
root_half = 0.7071067811865476
inv_root_two_pi = 0.3989422804014327
f32 = jnp.float32
bf16 = jnp.bfloat16
both_axes = ("slide", "tile")
lanes = 128
side = 32
rim = 3
taps = 7
row_block = 16
own_column = 8
wide = 48
vmem_limit = 58 * 1024 * 1024
middle_limit = vmem_limit
small_limit = vmem_limit


def swap(value, distance):
    pairs = [(d, d ^ distance) for d in range(lax.axis_size(both_axes))]
    return lax.ppermute(value, both_axes, pairs)


def pack_kernel(table_ref, tile_ref, out_ref, column_ref, edge_ref):
    me = lax.axis_index("tile")
    tiles = out_ref.shape[0]
    channels = tile_ref.shape[-1]
    for block in range(channels // lanes):
        here = pl.ds(block * lanes, lanes)
        for which, start, first in ((0, 0, 0), (1, 16, 13)):
            column_ref[...] = tile_ref[:, start : start + 16, here].astype(f32).reshape(16 * side, lanes)
            for c in range(rim):
                edge_ref[which, c, :, here] = column_ref[pl.ds(first + c, side, stride=16), :].astype(bf16)
    sources = (
        lambda: tile_ref[0:rim],
        lambda: tile_ref[side - rim : side],
        lambda: edge_ref[0],
        lambda: edge_ref[1],
    )
    for direction, source in enumerate((0, 1, 2, 3, 0, 0, 1, 1)):
        other = table_ref[0, me, direction]

        @pl.when(other < tiles)
        def _():
            out_ref[other] = sources[source]()


def pack_strips(table, tile):
    tiles = table.shape[1]
    channels = tile.shape[-1]
    return pl.pallas_call(
        pack_kernel,
        out_shape=jax.ShapeDtypeStruct((tiles, rim, side, channels), bf16),
        in_specs=[pl.BlockSpec(memory_space=pltpu.SMEM), pl.BlockSpec(memory_space=pltpu.VMEM)],
        out_specs=pl.BlockSpec(memory_space=pltpu.VMEM),
        scratch_shapes=[
            pltpu.VMEM((16 * side, lanes), f32),
            pltpu.VMEM((2, rim, side, channels), bf16),
        ],
        compiler_params=pltpu.CompilerParams(vmem_limit_bytes=small_limit),
        name="pack_strips",
    )(table, tile)


def assemble(table_ref, tile_ref, strip_ref, extended_ref):
    me = lax.axis_index("tile")
    tiles = strip_ref.shape[0]
    extended_ref[rim : rim + side, own_column : own_column + side, :] = tile_ref[...].astype(f32)

    def strip(direction):
        other = table_ref[0, me, direction]
        values = strip_ref[jnp.minimum(other, tiles - 1)].astype(f32)
        return jnp.where(other < tiles, values, jnp.zeros_like(values))

    last = rim + side
    right = own_column + side
    extended_ref[0:rim, own_column:right, :] = strip(0)
    extended_ref[last : last + rim, own_column:right, :] = strip(1)
    west = strip(2)
    east = strip(3)
    for c in range(rim):
        extended_ref[rim:last, own_column - rim + c, :] = west[c]
        extended_ref[rim:last, right + c, :] = east[c]
    extended_ref[0:rim, 0:8, :] = strip(4)[:, side - 8 :]
    extended_ref[0:rim, right : right + 8, :] = strip(5)[:, :8]
    extended_ref[last : last + rim, 0:8, :] = strip(6)[:, side - 8 :]
    extended_ref[last : last + rim, right : right + 8, :] = strip(7)[:, :8]


def spread_weights(weight_ref, spread_ref, flipped):
    for a in range(taps):
        rows = weight_ref[0, taps - 1 - a if flipped else a]
        for b in range(taps):
            at = taps - 1 - b if flipped else b
            spread_ref[b, a] = jnp.broadcast_to(rows[at : at + 1], (8, lanes))


def depthwise(extended_ref, spread_ref, store):
    def rows(block, carry):
        base = block * row_block
        for w in range(side // 8):
            totals = [None] * row_block
            for b in range(taps):
                start = own_column - rim + b + w * 8
                values = [extended_ref[base + r, start : start + 8, :] for r in range(row_block + taps - 1)]
                for a in range(taps):
                    factor = spread_ref[b, a]
                    for r in range(row_block):
                        term = values[r + a] * factor
                        totals[r] = term if totals[r] is None else totals[r] + term
            for r in range(row_block):
                store(base + r, w * 8, totals[r])
        return carry

    lax.fori_loop(0, side // row_block, rows, 0)


def inner_kernel(tile_ref, weight_ref, out_ref, extended_ref, spread_ref):
    @pl.when(pl.program_id(0) == 0)
    def _():
        extended_ref[...] = jnp.zeros_like(extended_ref)

    extended_ref[rim : rim + side, own_column : own_column + side, :] = tile_ref[...].astype(f32)
    spread_weights(weight_ref, spread_ref, False)

    def store(row, column, value):
        out_ref[0, row, column : column + 8, :] = value

    depthwise(extended_ref, spread_ref, store)


def conv_inner(tile, weight):
    channels = tile.shape[-1]
    blocks = channels // lanes
    return pl.pallas_call(
        inner_kernel,
        grid=(blocks,),
        out_shape=jax.ShapeDtypeStruct((blocks, side, side, lanes), f32),
        in_specs=[
            pl.BlockSpec((side, side, lanes), lambda i: (0, 0, i)),
            pl.BlockSpec((1, taps, taps, lanes), lambda i: (0, 0, 0, i)),
        ],
        out_specs=pl.BlockSpec((1, side, side, lanes), lambda i: (i, 0, 0, 0)),
        scratch_shapes=[
            pltpu.VMEM((side + 2 * rim, wide, lanes), f32),
            pltpu.VMEM((taps, taps, 8, lanes), f32),
        ],
        compiler_params=pltpu.CompilerParams(vmem_limit_bytes=small_limit),
        cost_estimate=pl.CostEstimate(flops=14_000_000_000, bytes_accessed=5_000_000, transcendentals=0),
        name="conv_inner",
    )(tile, weight)


def add_rim(table_ref, strip_ref, spread_ref, rows_ref, edge_ref, conv_ref, block):
    me = lax.axis_index("tile")
    tiles = strip_ref.shape[0]

    def strip(direction):
        other = table_ref[0, me, direction]
        values = strip_ref[jnp.minimum(other, tiles - 1)].astype(f32)
        return jnp.where(other < tiles, values, jnp.zeros_like(values))

    right = own_column + side
    for at, (middle, left, end) in enumerate(((0, 4, 5), (1, 6, 7))):
        rows_ref[at, :, own_column:right, :] = strip(middle)
        rows_ref[at, :, 0:8, :] = strip(left)[:, side - 8 :]
        rows_ref[at, :, right : right + 8, :] = strip(end)[:, :8]
    west, east = strip(2), strip(3)
    for c in range(rim):
        edge_ref[0, rim : rim + side, own_column - rim + c, :] = west[c]
        edge_ref[1, rim : rim + side, 8 + c, :] = east[c]

    for w in range(side // 8):
        for at, row, terms in (
            (0, 0, ((0, 0), (1, 1), (2, 2))),
            (0, 1, ((1, 0), (2, 1))),
            (0, 2, ((2, 0),)),
            (1, side - 1, ((0, 4), (1, 5), (2, 6))),
            (1, side - 2, ((0, 5), (1, 6))),
            (1, side - 3, ((0, 6),)),
        ):
            total = conv_ref[block, row, w * 8 : w * 8 + 8, :]
            for b in range(taps):
                start = own_column - rim + b + w * 8
                for source, a in terms:
                    total = total + rows_ref[at, source, start : start + 8, :] * spread_ref[b, a]
            conv_ref[block, row, w * 8 : w * 8 + 8, :] = total

    def columns(part, carry):
        base = part * row_block
        for which, w, picks in ((0, 0, ((0, 5), (1, 6), (2, 7))), (1, side // 8 - 1, ((4, 1), (5, 2), (6, 3)))):
            here = slice(w * 8, w * 8 + 8)
            totals = [conv_ref[block, base + r, here, :] for r in range(row_block)]
            for b, start in picks:
                values = [edge_ref[which, base + r, start : start + 8, :] for r in range(row_block + taps - 1)]
                for a in range(taps):
                    factor = spread_ref[b, a]
                    for r in range(row_block):
                        totals[r] = totals[r] + values[r + a] * factor
            for r in range(row_block):
                conv_ref[block, base + r, here, :] = totals[r]
        return carry

    lax.fori_loop(0, side // row_block, columns, 0)


def norm_kernel(
    table_ref, part_ref, strip_ref, weight_ref, gain_ref, shift_ref,
    whitened_ref, inv_ref, normed_ref, spread_ref, rows_ref, edge_ref, conv_ref,
):
    block = pl.program_id(0)
    blocks = whitened_ref.shape[1] // lanes

    @pl.when(block == 0)
    def _():
        edge_ref[...] = jnp.zeros_like(edge_ref)

    spread_weights(weight_ref, spread_ref, False)
    conv_ref[block] = part_ref[0]
    add_rim(table_ref, strip_ref, spread_ref, rows_ref, edge_ref, conv_ref, block)

    @pl.when(block == blocks - 1)
    def _():
        def norm(row, carry):
            parts = [conv_ref[j, row] for j in range(blocks)]
            count = blocks * lanes
            average = jnp.sum(sum(parts), axis=-1, keepdims=True) / count
            centred = [part - average for part in parts]
            spread = jnp.sum(sum(part * part for part in centred), axis=-1, keepdims=True) / count
            inv_std = lax.rsqrt(spread + ln_eps)
            here = pl.ds(pl.multiple_of(row * side, side), side)
            inv_ref[here, :] = inv_std
            for j in range(blocks):
                at = pl.ds(j * lanes, lanes)
                whitened = centred[j] * inv_std
                whitened_ref[here, at] = whitened
                normed_ref[here, at] = (whitened * gain_ref[:, at] + shift_ref[:, at]).astype(bf16)
            return carry

        lax.fori_loop(0, side, norm, 0, unroll=4)


def strip_spec(strips, first=0):
    return pl.BlockSpec((*strips.shape[:3], lanes), lambda i: (0, 0, 0, first + i))


def conv_norm(table, part, strips, weight, gain, shift):
    blocks = part.shape[0]
    channels = blocks * lanes
    pixels = side * side
    whole = lambda i: (0, 0)
    return pl.pallas_call(
        norm_kernel,
        grid=(blocks,),
        out_shape=[
            jax.ShapeDtypeStruct((pixels, channels), f32),
            jax.ShapeDtypeStruct((pixels, 1), f32),
            jax.ShapeDtypeStruct((pixels, channels), bf16),
        ],
        in_specs=[
            pl.BlockSpec(memory_space=pltpu.SMEM),
            pl.BlockSpec((1, side, side, lanes), lambda i: (i, 0, 0, 0)),
            strip_spec(strips),
            pl.BlockSpec((1, taps, taps, lanes), lambda i: (0, 0, 0, i)),
            pl.BlockSpec((1, channels), whole),
            pl.BlockSpec((1, channels), whole),
        ],
        out_specs=[full(pixels, channels), full(pixels, 1), full(pixels, channels)],
        scratch_shapes=[
            pltpu.VMEM((taps, taps, 8, lanes), f32),
            pltpu.VMEM((2, rim, wide, lanes), f32),
            pltpu.VMEM((2, side + 2 * rim, 16, lanes), f32),
            pltpu.VMEM((blocks, side, side, lanes), f32),
        ],
        compiler_params=pltpu.CompilerParams(vmem_limit_bytes=middle_limit),
        cost_estimate=pl.CostEstimate(flops=7_000_000_000, bytes_accessed=10_000_000, transcendentals=0),
        name="conv_norm",
    )(table, part, strips, weight, gain, shift)


dot = functools.partial(lax.dot_general, preferred_element_type=f32)
by_rows = (((1,), (1,)), ((), ()))
plain = (((1,), (0,)), ((), ()))
by_pixels = (((0,), (0,)), ((), ()))


def join_blocks(up_first_ref, up_second_ref, down_first_ref, down_second_ref, up_ref, down_ref):
    block = up_first_ref.shape[0]
    up_ref[:block] = up_first_ref[...]
    up_ref[block:] = up_second_ref[...]
    down_ref[:, :block] = down_first_ref[...]
    down_ref[:, block:] = down_second_ref[...]


def hidden_kernel(
    skip_ref, normed_ref, grad_ref, up_first_ref, up_second_ref, up_bias_ref, down_first_ref, down_second_ref,
    scale_ref,
    act_ref, pre_grad_ref, mine_ref, theirs_ref, bias_ref,
    branch_grad_ref, pair_ref, up_ref, down_ref,
):
    step = pl.program_id(0)
    pixels, channels = normed_ref.shape
    keep = (1 - skip_ref[0, 0]).astype(f32)
    tile_rows = 256
    join_blocks(up_first_ref, up_second_ref, down_first_ref, down_second_ref, up_ref, down_ref)

    @pl.when(step == 0)
    def _():
        branch_grad_ref[...] = (keep * scale_ref[...] * grad_ref[...].astype(f32)).astype(bf16)

    def rows_of(m):
        return pl.ds(m * tile_rows, tile_rows)

    def lift(m):
        return dot(normed_ref[rows_of(m), :], up_ref[...], by_rows) + up_bias_ref[0]

    bias_sum = jnp.zeros((1, up_ref.shape[0]), f32)
    count = pixels // tile_rows
    following = lift(0)
    for m in range(count):
        rows = rows_of(m)
        pre = following
        act_grad = dot(branch_grad_ref[rows, :], down_ref[...], plain)
        if m + 1 < count:
            following = lift(m + 1)
        cdf = 0.5 * (1.0 + lax.erf(pre * root_half))
        slope = cdf + pre * inv_root_two_pi * jnp.exp(-0.5 * pre * pre)
        act_ref[rows, :] = (pre * cdf).astype(bf16)
        pre_grad = (act_grad * slope).astype(bf16)
        pre_grad_ref[rows, :] = pre_grad
        bias_sum = bias_sum + jnp.sum(pre_grad.astype(f32), axis=0, keepdims=True)
    bias_ref[0] = bias_sum
    quarter = pair_ref.shape[1]
    left = dot(pre_grad_ref[...], normed_ref[...], by_pixels).astype(bf16)
    for q in range(4):
        pair_ref[q, :, :channels] = left[q * quarter : (q + 1) * quarter]
    right = dot(act_ref[...], branch_grad_ref[...], by_pixels).astype(bf16)
    for q in range(4):
        pair_ref[q, :, channels:] = right[q * quarter : (q + 1) * quarter]
    core = lax.axis_index("slide") % 2
    for high in range(2):
        mine_ref[0, high] = pair_ref[2 * high + core]
        theirs_ref[0, high] = pair_ref[2 * high + 1 - core]


once = pl.Buffered(1)
anywhere = pl.BlockSpec(memory_space=pl.ANY)
in_scalars = pl.BlockSpec(memory_space=pltpu.SMEM)


def full(*shape):
    return pl.BlockSpec(shape, lambda i: (0, 0), pipeline_mode=once)


def hidden_half(half, skip, normed, grad, up, up_bias, down, scale):
    pixels, channels = normed.shape
    hidden = up.shape[0]
    steps = 2
    chunk = hidden // 4
    quarter = chunk // 4
    block = chunk // 2
    part = jax.ShapeDtypeStruct((steps, 2, quarter, 2 * channels), bf16)
    part_spec = pl.BlockSpec((1, 2, quarter, 2 * channels), lambda i: (i, 0, 0, 0))
    wide_shape = jax.ShapeDtypeStruct((pixels, steps * chunk), bf16)
    wide_spec = pl.BlockSpec((pixels, chunk), lambda i: (0, i))
    return pl.pallas_call(
        hidden_kernel,
        grid=(steps,),
        out_shape=[wide_shape, wide_shape, part, part, jax.ShapeDtypeStruct((steps, 1, chunk), f32)],
        in_specs=[
            in_scalars,
            full(pixels, channels),
            full(pixels, channels),
            pl.BlockSpec((block, channels), lambda i: (4 * i + half, 0)),
            pl.BlockSpec((block, channels), lambda i: (4 * i + 2 + half, 0)),
            pl.BlockSpec((1, 1, chunk), lambda i: (2 * half + i, 0, 0)),
            pl.BlockSpec((channels, block), lambda i: (0, 4 * i + half)),
            pl.BlockSpec((channels, block), lambda i: (0, 4 * i + 2 + half)),
            full(1, channels),
        ],
        out_specs=[wide_spec, wide_spec, part_spec, part_spec, pl.BlockSpec((1, 1, chunk), lambda i: (i, 0, 0))],
        scratch_shapes=[
            pltpu.VMEM((pixels, channels), bf16),
            pltpu.VMEM((4, quarter, 2 * channels), bf16),
            pltpu.VMEM((chunk, channels), bf16),
            pltpu.VMEM((channels, chunk), bf16),
        ],
        compiler_params=pltpu.CompilerParams(vmem_limit_bytes=vmem_limit),
        cost_estimate=pl.CostEstimate(flops=14_000_000_000, bytes_accessed=20_000_000, transcendentals=0),
        name="hidden_half",
    )(skip, normed, grad, up, up, up_bias, down, down, scale)


def join_kernel(
    skip_ref, act_low_ref, act_high_ref, pre_low_ref, pre_high_ref,
    up_first_ref, up_second_ref, down_first_ref, down_second_ref, inv_ref, down_bias_ref, scale_ref, gain_ref, whitened_hbm_ref, tile_hbm_ref, grad_hbm_ref,
    out_ref, conv_grad_ref, channel_ref,
    branch_ref, normed_grad_ref, whitened_ref, tile_ref, grad_ref, arrived, up_ref, down_ref,
):
    step = pl.program_id(0)
    steps = pl.num_programs(0)
    pixels, channels = out_ref.shape
    pairs = ((whitened_hbm_ref, whitened_ref), (tile_hbm_ref, tile_ref), (grad_hbm_ref, grad_ref))
    copies = [pltpu.make_async_copy(*pair, arrived.at[at]) for at, pair in enumerate(pairs)]
    join_blocks(up_first_ref, up_second_ref, down_first_ref, down_second_ref, up_ref, down_ref)

    @pl.when(step == 0)
    def _():
        for copy in copies:
            copy.start()
        branch_ref[...] = dot(act_low_ref[...], down_ref[...], by_rows)
        normed_grad_ref[...] = dot(pre_low_ref[...], up_ref[...], plain)

    @pl.when(step == 1)
    def _():
        branch_ref[...] += dot(act_low_ref[...], down_ref[...], by_rows)
        normed_grad_ref[...] += dot(pre_low_ref[...], up_ref[...], plain)

    @pl.when(step >= 2)
    def _():
        branch_ref[...] += dot(act_high_ref[...], down_ref[...], by_rows)
        normed_grad_ref[...] += dot(pre_high_ref[...], up_ref[...], plain)

    @pl.when(step == steps - 1)
    def _():
        rows_each = 64
        keep = (1 - skip_ref[0, 0]).astype(f32)
        factor = keep * scale_ref[...]
        for copy in copies:
            copy.wait()

        def finish(m, sums):
            rows = pl.ds(pl.multiple_of(m * rows_each, rows_each), rows_each)
            grad = grad_ref[rows, :].astype(f32)
            branch = branch_ref[rows, :] + down_bias_ref[...]
            out_ref[rows, :] = (tile_ref[rows, :].astype(f32) + factor * branch).astype(bf16)
            whitened = whitened_ref[rows, :]
            normed_grad = normed_grad_ref[rows, :]
            scaled = normed_grad * gain_ref[...]
            product = normed_grad * whitened
            mean_one = jnp.sum(scaled, axis=-1, keepdims=True) / channels
            mean_two = jnp.sum(scaled * whitened, axis=-1, keepdims=True) / channels
            conv_grad = inv_ref[rows, :] * (scaled - mean_one - whitened * mean_two)
            conv_grad_ref[rows, :] = conv_grad.astype(bf16)
            branch_grad = (factor * grad).astype(bf16).astype(f32)
            terms = (product, normed_grad, branch_grad, grad * keep * branch)
            return tuple(
                total + jnp.sum(term.reshape(rows_each // 8, 8, channels), axis=0)
                for total, term in zip(sums, terms)
            )

        zero = jnp.zeros((8, channels), f32)
        sums = lax.fori_loop(0, pixels // rows_each, finish, (zero,) * 4, unroll=2)
        for at in range(4):
            channel_ref[at : at + 1, :] = jnp.sum(sums[at], axis=0, keepdims=True)


def join(skip, acts, pre_grads, up, down, inv_std, down_bias, scale, gain, whitened, tile, grad):
    pixels, channels = grad.shape
    chunk = acts[0].shape[1] // 2
    block = chunk // 2
    at_first = lambda i: 4 * (i % 2) + i // 2
    low_spec = pl.BlockSpec((pixels, chunk), lambda i: (0, jnp.minimum(i, 1)))
    high_spec = pl.BlockSpec((pixels, chunk), lambda i: (0, jnp.maximum(i - 2, 0)))
    pixel = jax.ShapeDtypeStruct((pixels, channels), bf16)
    return pl.pallas_call(
        join_kernel,
        grid=(4,),
        out_shape=[pixel, pixel, jax.ShapeDtypeStruct((4, channels), f32)],
        in_specs=[
            in_scalars,
            low_spec,
            high_spec,
            low_spec,
            high_spec,
            pl.BlockSpec((block, channels), lambda i: (at_first(i), 0)),
            pl.BlockSpec((block, channels), lambda i: (at_first(i) + 2, 0)),
            pl.BlockSpec((channels, block), lambda i: (0, at_first(i))),
            pl.BlockSpec((channels, block), lambda i: (0, at_first(i) + 2)),
            full(pixels, 1),
            full(1, channels),
            full(1, channels),
            full(1, channels),
            anywhere,
            anywhere,
            anywhere,
        ],
        out_specs=[full(pixels, channels), full(pixels, channels), full(4, channels)],
        scratch_shapes=[
            pltpu.VMEM((pixels, channels), f32),
            pltpu.VMEM((pixels, channels), f32),
            pltpu.VMEM((pixels, channels), f32),
            pltpu.VMEM((pixels, channels), bf16),
            pltpu.VMEM((pixels, channels), bf16),
            pltpu.SemaphoreType.DMA((3,)),
            pltpu.VMEM((chunk, channels), bf16),
            pltpu.VMEM((channels, chunk), bf16),
        ],
        compiler_params=pltpu.CompilerParams(vmem_limit_bytes=vmem_limit),
        cost_estimate=pl.CostEstimate(flops=14_000_000_000, bytes_accessed=30_000_000, transcendentals=0),
        name="join_halves",
    )(skip, *acts, *pre_grads, up, up, down, down, inv_std, down_bias, scale, gain, whitened, tile, grad)


def kernel_grad_kernel(table_ref, tile_ref, *refs):
    strip_ref, grad_ref, out_ref, extended_ref, wide_ref, total_ref = refs
    assemble(table_ref, tile_ref, strip_ref, extended_ref)
    wide_ref[...] = grad_ref[...].astype(f32)
    total_ref[...] = jnp.zeros_like(total_ref)

    def rows(block, carry):
        base = block * row_block
        for w in range(side // 8):
            grads = [wide_ref[base + r, w * 8 : w * 8 + 8, :] for r in range(row_block)]
            for b in range(taps):
                start = own_column - rim + b + w * 8
                values = [extended_ref[base + r, start : start + 8, :] for r in range(row_block + taps - 1)]
                for a in range(taps):
                    terms = [values[r + a] * grads[r] for r in range(row_block)]
                    while len(terms) > 1:
                        terms = [terms[i] + terms[i + 1] for i in range(0, len(terms), 2)]
                    total_ref[a, b] += terms[0]
        return carry

    lax.fori_loop(0, side // row_block, rows, 0)
    for a in range(taps):
        out_ref[a] = jnp.sum(total_ref[a], axis=1)


def kernel_grad(table, tile, strips, conv_grad):
    channels = tile.shape[-1]
    block_spec = pl.BlockSpec((side, side, lanes), lambda i: (0, 0, i))
    return pl.pallas_call(
        kernel_grad_kernel,
        grid=(channels // lanes,),
        out_shape=jax.ShapeDtypeStruct((taps, taps, channels), f32),
        in_specs=[pl.BlockSpec(memory_space=pltpu.SMEM), block_spec, strip_spec(strips), block_spec],
        out_specs=pl.BlockSpec((taps, taps, lanes), lambda i: (0, 0, i)),
        scratch_shapes=[
            pltpu.VMEM((side + 2 * rim, wide, lanes), f32),
            pltpu.VMEM((side, side, lanes), f32),
            pltpu.VMEM((taps, taps, 8, lanes), f32),
        ],
        compiler_params=pltpu.CompilerParams(vmem_limit_bytes=small_limit),
        cost_estimate=pl.CostEstimate(flops=14_000_000_000, bytes_accessed=5_000_000, transcendentals=0),
        name="kernel_grad",
    )(table, tile, strips, conv_grad)


def back_kernel(table_ref, tile_ref, *refs):
    strip_ref, weight_ref, grad_ref = refs[:3]
    out_ref, extended_ref, spread_ref, total_ref = refs[-4:]
    assemble(table_ref, tile_ref, strip_ref, extended_ref)
    spread_weights(weight_ref, spread_ref, True)

    def store(row, column, value):
        total_ref[row, column : column + 8, :] = value

    depthwise(extended_ref, spread_ref, store)
    out_ref[...] = (grad_ref[...].astype(f32) + total_ref[...]).astype(bf16)


def back_conv(table, tile, strips, weight, grad, part, parts, done=None):
    channels = tile.shape[-1]
    steps = channels // lanes // parts
    first = part * steps
    block_spec = pl.BlockSpec((side, side, lanes), lambda i: (0, 0, first + i))
    earlier = [] if done is None else [done]
    return pl.pallas_call(
        back_kernel,
        grid=(steps,),
        out_shape=jax.ShapeDtypeStruct(tile.shape, bf16),
        in_specs=[
            pl.BlockSpec(memory_space=pltpu.SMEM),
            block_spec,
            strip_spec(strips, first),
            pl.BlockSpec((1, taps, taps, lanes), lambda i: (0, 0, 0, first + i)),
            block_spec,
            *[pl.BlockSpec(memory_space=pl.ANY) for _ in earlier],
        ],
        out_specs=block_spec,
        scratch_shapes=[
            pltpu.VMEM((side + 2 * rim, wide, lanes), f32),
            pltpu.VMEM((taps, taps, 8, lanes), f32),
            pltpu.VMEM((side, side, lanes), f32),
        ],
        input_output_aliases={5: 0} if earlier else {},
        compiler_params=pltpu.CompilerParams(vmem_limit_bytes=small_limit),
        cost_estimate=pl.CostEstimate(
            flops=14_000_000_000 // parts, bytes_accessed=5_000_000 // parts, transcendentals=0
        ),
        name="back_conv",
    )(table, tile, strips, weight, grad, *earlier)


def pick(value, positions):
    for axis, index in positions:
        value = lax.dynamic_index_in_dim(value, index, axis, keepdims=False)
    return value


def fold(parts, dtype):
    wide_parts = [part.astype(f32) for part in parts]
    while len(wide_parts) > 1:
        wide_parts = [wide_parts[i] + wide_parts[i + 1] for i in range(0, len(wide_parts), 2)]
    return wide_parts[0].astype(dtype)


def reduce_axis(take, distance, dtype):
    kept = take(0)
    arrived = [swap(take(k), k * distance) for k in (1, 2, 3)]
    return fold([kept, *arrived], dtype)


def place():
    slide, tile = lax.axis_index("slide"), lax.axis_index("tile")
    return slide // 4, (slide // 2) % 2, tile // 4, tile % 4


def x_parts(value):
    x = place()[3]
    return [pick(value, [(value.ndim - 3, x ^ k)]) for k in range(4)]


def y_parts(value):
    _, y_hi, y_lo, _ = place()
    return [pick(value, [(1, y_lo ^ (k % 2)), (0, y_hi ^ (k // 2))]) for k in range(4)]


def z_parts(value):
    z = place()[0]
    return [pick(value, [(0, z ^ k)]) for k in range(4)]


x_distances = (1, 2, 3)
y_distances = (4, 16, 20)
z_distances = (32, 64, 96)


def gather_sum(parts, distances, dtype, ready):
    arrived = [swap(part, d) for part, d in zip(parts[1:], distances)]
    return fold(gate([parts[0], *arrived], ready), dtype)


def gate(values, ready):
    return list(lax.optimization_barrier((*values, ready))[: len(values)])


def after(value, *others):
    return lax.optimization_barrier((value, *others))[0]


def trade(value, distance, ready):
    value, arrived = gate([value, swap(value, distance)], ready)
    return value + arrived


def ride(parts, small):
    width = parts[0].shape[-1]
    extra = small.astype(bf16).reshape(-1, width)
    sent = [jnp.concatenate([part.reshape(-1, width), extra], 0) for part in parts[1:]]
    return sent, lax.reduce_precision(small, 8, 7)


def land(sent, small, parts, distances, dtype, ready):
    arrived = [swap(value, d) for value, d in zip(sent, distances)]
    size = parts[0].size // parts[0].shape[-1]
    mine, small, *arrived = gate([parts[0], small, *arrived], ready)
    total = fold([mine, *[value[:size].reshape(mine.shape) for value in arrived]], dtype)
    return total, fold([small, *[value[size:].reshape(small.shape) for value in arrived]], f32)


def on_device(
    features,
    cotangent,
    neighbours,
    skip_flags,
    dw_weight,
    ln_gain,
    ln_bias,
    up_weight,
    up_bias,
    down_weight,
    down_bias,
    layer_scale,
):
    channels = features.shape[-1]
    hidden = up_weight.shape[1]
    tile = features[0, 0]
    grad = cotangent[0, 0]
    flat = (side * side, channels)
    packed = pack_strips(neighbours, tile)
    strips = lax.all_to_all(packed, "tile", 0, 0)
    inner = conv_inner(after(tile, packed), dw_weight)
    strips = after(strips, inner)
    whitened, inv_std, normed = conv_norm(neighbours, inner, strips, dw_weight, ln_gain, ln_bias)
    flat_grad = grad.reshape(flat)
    bias_order = jnp.swapaxes(up_bias.reshape(4, 2, -1), 0, 1).reshape(4, 1, -1)
    mlp_in = (flat_grad, up_weight[0], bias_order, down_weight[0], layer_scale)
    act_low, pre_low, mine_low, theirs_low, bias_low = hidden_half(0, skip_flags, normed, *mlp_in)
    received_low = swap(theirs_low, 8)
    act_high, pre_high, mine_high, theirs_high, bias_high = hidden_half(1, skip_flags, after(normed, theirs_low), *mlp_in)
    rows = mine_low.shape[2] // 8
    width = mine_low.shape[3]
    grid = (4, 2, 4, rows, width)
    received_high = swap(theirs_high, 8)
    low_x = x_parts(fold(gate([mine_low, received_low], act_high), bf16).reshape(grid))
    high_z = z_parts(fold([mine_high, received_high], bf16).reshape(grid))
    got_high = [swap(high_z[1], 32), swap(high_z[3], 96)]
    out, conv_grad, channel_sums = join(
        skip_flags, (after(act_low, *low_x, *high_z), act_high), (pre_low, pre_high), up_weight[0], down_weight[0],
        inv_std, down_bias, layer_scale, ln_gain, whitened, tile.reshape(flat), flat_grad,
    )
    got_far = swap(after(high_z[2], conv_grad), 64)
    conv_grad = conv_grad.reshape(tile.shape)
    packed = pack_strips(neighbours, conv_grad)
    grad_strips = lax.all_to_all(packed, "tile", 0, 0)
    first, second, third = gate([high_z[0], *got_high], packed)
    near = first.astype(f32) + second.astype(f32) + third.astype(f32)
    low_z = z_parts(gather_sum(low_x, x_distances, bf16, packed))
    kernel_sums = kernel_grad(neighbours, tile, strips, after(conv_grad, near, *low_z))
    small = jnp.concatenate(
        [
            kernel_sums.reshape(taps * taps, channels),
            channel_sums,
            jnp.stack([bias_low.reshape(4, -1), bias_high.reshape(4, -1)], 1).reshape(-1, channels),
        ],
        0,
    )
    count = small.shape[0]
    small = jnp.pad(small, ((0, -count % 16), (0, 0)))
    done_low = gather_sum(low_z, z_distances, bf16, kernel_sums)
    high_x = x_parts(fold(gate([near, got_far], done_low), bf16))
    back = functools.partial(back_conv, neighbours)
    grad_strips = after(grad_strips, small)
    wide_x, small = ride(high_x, small)
    input_grad = back(after(conv_grad, *wide_x), grad_strips, dw_weight, grad, 0, 3)
    done_high, small = land(wide_x, small, high_x, x_distances, bf16, input_grad)
    last = y_parts(jnp.concatenate([done_low, done_high], 0).reshape(2, 2, rows, width))
    wide_y, small = ride(last, small)
    input_grad = back(after(conv_grad, *wide_y), grad_strips, dw_weight, grad, 1, 3, input_grad)
    weight_rows, small = land(wide_y, small, last, y_distances, f32, input_grad)
    sent_small = small.astype(bf16)
    got_small = [swap(sent_small, d) for d in z_distances]
    input_grad = back(after(conv_grad, sent_small), grad_strips, dw_weight, grad, 2, 3, input_grad)
    small = fold(gate([lax.reduce_precision(small, 8, 7), *got_small], input_grad), f32)
    small = trade(small, 8, small)[:count]
    split = taps * taps
    return (
        out.reshape(features.shape),
        input_grad[None, None],
        weight_rows[None],
        small[:split].reshape(1, taps, taps, channels),
        small[split : split + 4][None],
        small[split + 4 :].reshape(1, hidden),
    )


def solution(mesh):
    return jax.shard_map(
        on_device,
        mesh=mesh,
        in_specs=(
            P("slide", "tile", None, None, None),
            P("slide", "tile", None, None, None),
            P("slide", None, None),
            P(None, "slide"),
            P(),
            P(),
            P(),
            P(),
            P(),
            P(),
            P(),
            P(),
        ),
        out_specs=(
            P("slide", "tile", None, None, None),
            P("slide", "tile", None, None, None),
            P(None, ("slide", "tile"), None),
            P(),
            P(),
            P(),
        ),
        check_vma=False,
    )
```

```python
import functools

import jax
import jax.numpy as jnp
from jax import lax
from jax.experimental import pallas as pl
from jax.experimental.pallas import tpu as pltpu
from jax.sharding import PartitionSpec as P

ln_eps = 1e-06
root_half = 0.7071067811865476
inv_root_two_pi = 0.3989422804014327
f32 = jnp.float32
bf16 = jnp.bfloat16
both_axes = ("slide", "tile")
lanes = 128
side = 32
rim = 3
taps = 7
row_block = 16
own_column = 8
wide = 48
vmem_limit = 58 * 1024 * 1024
middle_limit = vmem_limit
small_limit = vmem_limit


def swap(value, distance):
    pairs = [(d, d ^ distance) for d in range(lax.axis_size(both_axes))]
    return lax.ppermute(value, both_axes, pairs)


def pack_kernel(table_ref, tile_ref, out_ref, column_ref, edge_ref):
    me = lax.axis_index("tile")
    tiles = out_ref.shape[0]
    channels = tile_ref.shape[-1]
    for block in range(channels // lanes):
        here = pl.ds(block * lanes, lanes)
        for which, start, first in ((0, 0, 0), (1, 16, 13)):
            column_ref[...] = tile_ref[:, start : start + 16, here].astype(f32).reshape(16 * side, lanes)
            for c in range(rim):
                edge_ref[which, c, :, here] = column_ref[pl.ds(first + c, side, stride=16), :].astype(bf16)
    sources = (
        lambda: tile_ref[0:rim],
        lambda: tile_ref[side - rim : side],
        lambda: edge_ref[0],
        lambda: edge_ref[1],
    )
    for direction, source in enumerate((0, 1, 2, 3, 0, 0, 1, 1)):
        other = table_ref[0, me, direction]

        @pl.when(other < tiles)
        def _():
            out_ref[other] = sources[source]()


def pack_strips(table, tile):
    tiles = table.shape[1]
    channels = tile.shape[-1]
    return pl.pallas_call(
        pack_kernel,
        out_shape=jax.ShapeDtypeStruct((tiles, rim, side, channels), bf16),
        in_specs=[pl.BlockSpec(memory_space=pltpu.SMEM), pl.BlockSpec(memory_space=pltpu.VMEM)],
        out_specs=pl.BlockSpec(memory_space=pltpu.VMEM),
        scratch_shapes=[
            pltpu.VMEM((16 * side, lanes), f32),
            pltpu.VMEM((2, rim, side, channels), bf16),
        ],
        compiler_params=pltpu.CompilerParams(vmem_limit_bytes=small_limit),
        name="pack_strips",
    )(table, tile)


def assemble(table_ref, tile_ref, strip_ref, extended_ref):
    me = lax.axis_index("tile")
    tiles = strip_ref.shape[0]
    extended_ref[rim : rim + side, own_column : own_column + side, :] = tile_ref[...].astype(f32)

    def strip(direction):
        other = table_ref[0, me, direction]
        values = strip_ref[jnp.minimum(other, tiles - 1)].astype(f32)
        return jnp.where(other < tiles, values, jnp.zeros_like(values))

    last = rim + side
    right = own_column + side
    extended_ref[0:rim, own_column:right, :] = strip(0)
    extended_ref[last : last + rim, own_column:right, :] = strip(1)
    west = strip(2)
    east = strip(3)
    for c in range(rim):
        extended_ref[rim:last, own_column - rim + c, :] = west[c]
        extended_ref[rim:last, right + c, :] = east[c]
    extended_ref[0:rim, 0:8, :] = strip(4)[:, side - 8 :]
    extended_ref[0:rim, right : right + 8, :] = strip(5)[:, :8]
    extended_ref[last : last + rim, 0:8, :] = strip(6)[:, side - 8 :]
    extended_ref[last : last + rim, right : right + 8, :] = strip(7)[:, :8]


def spread_weights(weight_ref, spread_ref, flipped):
    for a in range(taps):
        rows = weight_ref[0, taps - 1 - a if flipped else a]
        for b in range(taps):
            at = taps - 1 - b if flipped else b
            spread_ref[b, a] = jnp.broadcast_to(rows[at : at + 1], (8, lanes))


def depthwise(extended_ref, spread_ref, store):
    def rows(block, carry):
        base = block * row_block
        for w in range(side // 8):
            totals = [None] * row_block
            for b in range(taps):
                start = own_column - rim + b + w * 8
                values = [extended_ref[base + r, start : start + 8, :] for r in range(row_block + taps - 1)]
                for a in range(taps):
                    factor = spread_ref[b, a]
                    for r in range(row_block):
                        term = values[r + a] * factor
                        totals[r] = term if totals[r] is None else totals[r] + term
            for r in range(row_block):
                store(base + r, w * 8, totals[r])
        return carry

    lax.fori_loop(0, side // row_block, rows, 0)


def inner_kernel(tile_ref, weight_ref, out_ref, extended_ref, spread_ref):
    @pl.when(pl.program_id(0) == 0)
    def _():
        extended_ref[...] = jnp.zeros_like(extended_ref)

    extended_ref[rim : rim + side, own_column : own_column + side, :] = tile_ref[...].astype(f32)
    spread_weights(weight_ref, spread_ref, False)

    def store(row, column, value):
        out_ref[0, row, column : column + 8, :] = value

    depthwise(extended_ref, spread_ref, store)


def conv_inner(tile, weight):
    channels = tile.shape[-1]
    blocks = channels // lanes
    return pl.pallas_call(
        inner_kernel,
        grid=(blocks,),
        out_shape=jax.ShapeDtypeStruct((blocks, side, side, lanes), f32),
        in_specs=[
            pl.BlockSpec((side, side, lanes), lambda i: (0, 0, i)),
            pl.BlockSpec((1, taps, taps, lanes), lambda i: (0, 0, 0, i)),
        ],
        out_specs=pl.BlockSpec((1, side, side, lanes), lambda i: (i, 0, 0, 0)),
        scratch_shapes=[
            pltpu.VMEM((side + 2 * rim, wide, lanes), f32),
            pltpu.VMEM((taps, taps, 8, lanes), f32),
        ],
        compiler_params=pltpu.CompilerParams(vmem_limit_bytes=small_limit),
        cost_estimate=pl.CostEstimate(flops=14_000_000_000, bytes_accessed=5_000_000, transcendentals=0),
        name="conv_inner",
    )(tile, weight)


def add_rim(table_ref, strip_ref, spread_ref, rows_ref, edge_ref, conv_ref, block):
    me = lax.axis_index("tile")
    tiles = strip_ref.shape[0]

    def strip(direction):
        other = table_ref[0, me, direction]
        values = strip_ref[jnp.minimum(other, tiles - 1)].astype(f32)
        return jnp.where(other < tiles, values, jnp.zeros_like(values))

    right = own_column + side
    for at, (middle, left, end) in enumerate(((0, 4, 5), (1, 6, 7))):
        rows_ref[at, :, own_column:right, :] = strip(middle)
        rows_ref[at, :, 0:8, :] = strip(left)[:, side - 8 :]
        rows_ref[at, :, right : right + 8, :] = strip(end)[:, :8]
    west, east = strip(2), strip(3)
    for c in range(rim):
        edge_ref[0, rim : rim + side, own_column - rim + c, :] = west[c]
        edge_ref[1, rim : rim + side, 8 + c, :] = east[c]

    for w in range(side // 8):
        for at, row, terms in (
            (0, 0, ((0, 0), (1, 1), (2, 2))),
            (0, 1, ((1, 0), (2, 1))),
            (0, 2, ((2, 0),)),
            (1, side - 1, ((0, 4), (1, 5), (2, 6))),
            (1, side - 2, ((0, 5), (1, 6))),
            (1, side - 3, ((0, 6),)),
        ):
            total = conv_ref[block, row, w * 8 : w * 8 + 8, :]
            for b in range(taps):
                start = own_column - rim + b + w * 8
                for source, a in terms:
                    total = total + rows_ref[at, source, start : start + 8, :] * spread_ref[b, a]
            conv_ref[block, row, w * 8 : w * 8 + 8, :] = total

    def columns(part, carry):
        base = part * row_block
        for which, w, picks in ((0, 0, ((0, 5), (1, 6), (2, 7))), (1, side // 8 - 1, ((4, 1), (5, 2), (6, 3)))):
            here = slice(w * 8, w * 8 + 8)
            totals = [conv_ref[block, base + r, here, :] for r in range(row_block)]
            for b, start in picks:
                values = [edge_ref[which, base + r, start : start + 8, :] for r in range(row_block + taps - 1)]
                for a in range(taps):
                    factor = spread_ref[b, a]
                    for r in range(row_block):
                        totals[r] = totals[r] + values[r + a] * factor
            for r in range(row_block):
                conv_ref[block, base + r, here, :] = totals[r]
        return carry

    lax.fori_loop(0, side // row_block, columns, 0)


def norm_kernel(
    table_ref, part_ref, strip_ref, weight_ref, gain_ref, shift_ref,
    whitened_ref, inv_ref, normed_ref, spread_ref, rows_ref, edge_ref, conv_ref,
):
    block = pl.program_id(0)
    blocks = whitened_ref.shape[1] // lanes

    @pl.when(block == 0)
    def _():
        edge_ref[...] = jnp.zeros_like(edge_ref)

    spread_weights(weight_ref, spread_ref, False)
    conv_ref[block] = part_ref[0]
    add_rim(table_ref, strip_ref, spread_ref, rows_ref, edge_ref, conv_ref, block)

    @pl.when(block == blocks - 1)
    def _():
        def norm(row, carry):
            parts = [conv_ref[j, row] for j in range(blocks)]
            count = blocks * lanes
            average = jnp.sum(sum(parts), axis=-1, keepdims=True) / count
            centred = [part - average for part in parts]
            spread = jnp.sum(sum(part * part for part in centred), axis=-1, keepdims=True) / count
            inv_std = lax.rsqrt(spread + ln_eps)
            here = pl.ds(pl.multiple_of(row * side, side), side)
            inv_ref[here, :] = inv_std
            for j in range(blocks):
                at = pl.ds(j * lanes, lanes)
                whitened = centred[j] * inv_std
                whitened_ref[here, at] = whitened
                normed_ref[here, at] = (whitened * gain_ref[:, at] + shift_ref[:, at]).astype(bf16)
            return carry

        lax.fori_loop(0, side, norm, 0, unroll=4)


def strip_spec(strips, first=0):
    return pl.BlockSpec((*strips.shape[:3], lanes), lambda i: (0, 0, 0, first + i))


def conv_norm(table, part, strips, weight, gain, shift):
    blocks = part.shape[0]
    channels = blocks * lanes
    pixels = side * side
    whole = lambda i: (0, 0)
    return pl.pallas_call(
        norm_kernel,
        grid=(blocks,),
        out_shape=[
            jax.ShapeDtypeStruct((pixels, channels), f32),
            jax.ShapeDtypeStruct((pixels, 1), f32),
            jax.ShapeDtypeStruct((pixels, channels), bf16),
        ],
        in_specs=[
            pl.BlockSpec(memory_space=pltpu.SMEM),
            pl.BlockSpec((1, side, side, lanes), lambda i: (i, 0, 0, 0)),
            strip_spec(strips),
            pl.BlockSpec((1, taps, taps, lanes), lambda i: (0, 0, 0, i)),
            pl.BlockSpec((1, channels), whole),
            pl.BlockSpec((1, channels), whole),
        ],
        out_specs=[full(pixels, channels), full(pixels, 1), full(pixels, channels)],
        scratch_shapes=[
            pltpu.VMEM((taps, taps, 8, lanes), f32),
            pltpu.VMEM((2, rim, wide, lanes), f32),
            pltpu.VMEM((2, side + 2 * rim, 16, lanes), f32),
            pltpu.VMEM((blocks, side, side, lanes), f32),
        ],
        compiler_params=pltpu.CompilerParams(vmem_limit_bytes=middle_limit),
        cost_estimate=pl.CostEstimate(flops=7_000_000_000, bytes_accessed=10_000_000, transcendentals=0),
        name="conv_norm",
    )(table, part, strips, weight, gain, shift)


dot = functools.partial(lax.dot_general, preferred_element_type=f32)
by_rows = (((1,), (1,)), ((), ()))
plain = (((1,), (0,)), ((), ()))
by_pixels = (((0,), (0,)), ((), ()))


def join_blocks(up_first_ref, up_second_ref, down_first_ref, down_second_ref, up_ref, down_ref):
    block = up_first_ref.shape[0]
    up_ref[:block] = up_first_ref[...]
    up_ref[block:] = up_second_ref[...]
    down_ref[:, :block] = down_first_ref[...]
    down_ref[:, block:] = down_second_ref[...]


def hidden_kernel(
    skip_ref, normed_ref, grad_ref, up_first_ref, up_second_ref, up_bias_ref, down_first_ref, down_second_ref,
    scale_ref,
    act_ref, pre_grad_ref, mine_ref, theirs_ref, bias_ref,
    branch_grad_ref, pair_ref, up_ref, down_ref,
):
    step = pl.program_id(0)
    pixels, channels = normed_ref.shape
    keep = (1 - skip_ref[0, 0]).astype(f32)
    tile_rows = 256
    join_blocks(up_first_ref, up_second_ref, down_first_ref, down_second_ref, up_ref, down_ref)

    @pl.when(step == 0)
    def _():
        branch_grad_ref[...] = (keep * scale_ref[...] * grad_ref[...].astype(f32)).astype(bf16)

    def rows_of(m):
        return pl.ds(m * tile_rows, tile_rows)

    def lift(m):
        return dot(normed_ref[rows_of(m), :], up_ref[...], by_rows) + up_bias_ref[0]

    bias_sum = jnp.zeros((1, up_ref.shape[0]), f32)
    count = pixels // tile_rows
    following = lift(0)
    for m in range(count):
        rows = rows_of(m)
        pre = following
        act_grad = dot(branch_grad_ref[rows, :], down_ref[...], plain)
        if m + 1 < count:
            following = lift(m + 1)
        cdf = 0.5 * (1.0 + lax.erf(pre * root_half))
        slope = cdf + pre * inv_root_two_pi * jnp.exp(-0.5 * pre * pre)
        act_ref[rows, :] = (pre * cdf).astype(bf16)
        pre_grad = (act_grad * slope).astype(bf16)
        pre_grad_ref[rows, :] = pre_grad
        bias_sum = bias_sum + jnp.sum(pre_grad.astype(f32), axis=0, keepdims=True)
    bias_ref[0] = bias_sum
    quarter = pair_ref.shape[1]
    left = dot(pre_grad_ref[...], normed_ref[...], by_pixels).astype(bf16)
    for q in range(4):
        pair_ref[q, :, :channels] = left[q * quarter : (q + 1) * quarter]
    right = dot(act_ref[...], branch_grad_ref[...], by_pixels).astype(bf16)
    for q in range(4):
        pair_ref[q, :, channels:] = right[q * quarter : (q + 1) * quarter]
    core = lax.axis_index("slide") % 2
    for high in range(2):
        mine_ref[0, high] = pair_ref[2 * high + core]
        theirs_ref[0, high] = pair_ref[2 * high + 1 - core]


once = pl.Buffered(1)
anywhere = pl.BlockSpec(memory_space=pl.ANY)
in_scalars = pl.BlockSpec(memory_space=pltpu.SMEM)


def full(*shape):
    return pl.BlockSpec(shape, lambda i: (0, 0), pipeline_mode=once)


def hidden_half(half, skip, normed, grad, up, up_bias, down, scale):
    pixels, channels = normed.shape
    hidden = up.shape[0]
    steps = 2
    chunk = hidden // 4
    quarter = chunk // 4
    block = chunk // 2
    part = jax.ShapeDtypeStruct((steps, 2, quarter, 2 * channels), bf16)
    part_spec = pl.BlockSpec((1, 2, quarter, 2 * channels), lambda i: (i, 0, 0, 0))
    wide_shape = jax.ShapeDtypeStruct((pixels, steps * chunk), bf16)
    wide_spec = pl.BlockSpec((pixels, chunk), lambda i: (0, i))
    return pl.pallas_call(
        hidden_kernel,
        grid=(steps,),
        out_shape=[wide_shape, wide_shape, part, part, jax.ShapeDtypeStruct((steps, 1, chunk), f32)],
        in_specs=[
            in_scalars,
            full(pixels, channels),
            full(pixels, channels),
            pl.BlockSpec((block, channels), lambda i: (4 * i + half, 0)),
            pl.BlockSpec((block, channels), lambda i: (4 * i + 2 + half, 0)),
            pl.BlockSpec((1, 1, chunk), lambda i: (2 * half + i, 0, 0)),
            pl.BlockSpec((channels, block), lambda i: (0, 4 * i + half)),
            pl.BlockSpec((channels, block), lambda i: (0, 4 * i + 2 + half)),
            full(1, channels),
        ],
        out_specs=[wide_spec, wide_spec, part_spec, part_spec, pl.BlockSpec((1, 1, chunk), lambda i: (i, 0, 0))],
        scratch_shapes=[
            pltpu.VMEM((pixels, channels), bf16),
            pltpu.VMEM((4, quarter, 2 * channels), bf16),
            pltpu.VMEM((chunk, channels), bf16),
            pltpu.VMEM((channels, chunk), bf16),
        ],
        compiler_params=pltpu.CompilerParams(vmem_limit_bytes=vmem_limit),
        cost_estimate=pl.CostEstimate(flops=14_000_000_000, bytes_accessed=20_000_000, transcendentals=0),
        name="hidden_half",
    )(skip, normed, grad, up, up, up_bias, down, down, scale)


def join_kernel(
    skip_ref, act_low_ref, act_high_ref, pre_low_ref, pre_high_ref,
    up_first_ref, up_second_ref, down_first_ref, down_second_ref, inv_ref, down_bias_ref, scale_ref, gain_ref, whitened_hbm_ref, tile_hbm_ref, grad_hbm_ref,
    out_ref, conv_grad_ref, channel_ref,
    branch_ref, normed_grad_ref, whitened_ref, tile_ref, grad_ref, arrived, up_ref, down_ref,
):
    step = pl.program_id(0)
    steps = pl.num_programs(0)
    pixels, channels = out_ref.shape
    pairs = ((whitened_hbm_ref, whitened_ref), (tile_hbm_ref, tile_ref), (grad_hbm_ref, grad_ref))
    copies = [pltpu.make_async_copy(*pair, arrived.at[at]) for at, pair in enumerate(pairs)]
    join_blocks(up_first_ref, up_second_ref, down_first_ref, down_second_ref, up_ref, down_ref)

    @pl.when(step == 0)
    def _():
        for copy in copies:
            copy.start()
        branch_ref[...] = dot(act_low_ref[...], down_ref[...], by_rows)
        normed_grad_ref[...] = dot(pre_low_ref[...], up_ref[...], plain)

    @pl.when(step == 1)
    def _():
        branch_ref[...] += dot(act_low_ref[...], down_ref[...], by_rows)
        normed_grad_ref[...] += dot(pre_low_ref[...], up_ref[...], plain)

    @pl.when(step >= 2)
    def _():
        branch_ref[...] += dot(act_high_ref[...], down_ref[...], by_rows)
        normed_grad_ref[...] += dot(pre_high_ref[...], up_ref[...], plain)

    @pl.when(step == steps - 1)
    def _():
        rows_each = 64
        keep = (1 - skip_ref[0, 0]).astype(f32)
        factor = keep * scale_ref[...]
        for copy in copies:
            copy.wait()

        def finish(m, sums):
            rows = pl.ds(pl.multiple_of(m * rows_each, rows_each), rows_each)
            grad = grad_ref[rows, :].astype(f32)
            branch = branch_ref[rows, :] + down_bias_ref[...]
            out_ref[rows, :] = (tile_ref[rows, :].astype(f32) + factor * branch).astype(bf16)
            whitened = whitened_ref[rows, :]
            normed_grad = normed_grad_ref[rows, :]
            scaled = normed_grad * gain_ref[...]
            product = normed_grad * whitened
            mean_one = jnp.sum(scaled, axis=-1, keepdims=True) / channels
            mean_two = jnp.sum(scaled * whitened, axis=-1, keepdims=True) / channels
            conv_grad = inv_ref[rows, :] * (scaled - mean_one - whitened * mean_two)
            conv_grad_ref[rows, :] = conv_grad.astype(bf16)
            branch_grad = (factor * grad).astype(bf16).astype(f32)
            terms = (product, normed_grad, branch_grad, grad * keep * branch)
            return tuple(
                total + jnp.sum(term.reshape(rows_each // 8, 8, channels), axis=0)
                for total, term in zip(sums, terms)
            )

        zero = jnp.zeros((8, channels), f32)
        sums = lax.fori_loop(0, pixels // rows_each, finish, (zero,) * 4, unroll=2)
        for at in range(4):
            channel_ref[at : at + 1, :] = jnp.sum(sums[at], axis=0, keepdims=True)


def join(skip, acts, pre_grads, up, down, inv_std, down_bias, scale, gain, whitened, tile, grad):
    pixels, channels = grad.shape
    chunk = acts[0].shape[1] // 2
    block = chunk // 2
    at_first = lambda i: 4 * (i % 2) + i // 2
    low_spec = pl.BlockSpec((pixels, chunk), lambda i: (0, jnp.minimum(i, 1)))
    high_spec = pl.BlockSpec((pixels, chunk), lambda i: (0, jnp.maximum(i - 2, 0)))
    pixel = jax.ShapeDtypeStruct((pixels, channels), bf16)
    return pl.pallas_call(
        join_kernel,
        grid=(4,),
        out_shape=[pixel, pixel, jax.ShapeDtypeStruct((4, channels), f32)],
        in_specs=[
            in_scalars,
            low_spec,
            high_spec,
            low_spec,
            high_spec,
            pl.BlockSpec((block, channels), lambda i: (at_first(i), 0)),
            pl.BlockSpec((block, channels), lambda i: (at_first(i) + 2, 0)),
            pl.BlockSpec((channels, block), lambda i: (0, at_first(i))),
            pl.BlockSpec((channels, block), lambda i: (0, at_first(i) + 2)),
            full(pixels, 1),
            full(1, channels),
            full(1, channels),
            full(1, channels),
            anywhere,
            anywhere,
            anywhere,
        ],
        out_specs=[full(pixels, channels), full(pixels, channels), full(4, channels)],
        scratch_shapes=[
            pltpu.VMEM((pixels, channels), f32),
            pltpu.VMEM((pixels, channels), f32),
            pltpu.VMEM((pixels, channels), f32),
            pltpu.VMEM((pixels, channels), bf16),
            pltpu.VMEM((pixels, channels), bf16),
            pltpu.SemaphoreType.DMA((3,)),
            pltpu.VMEM((chunk, channels), bf16),
            pltpu.VMEM((channels, chunk), bf16),
        ],
        compiler_params=pltpu.CompilerParams(vmem_limit_bytes=vmem_limit),
        cost_estimate=pl.CostEstimate(flops=14_000_000_000, bytes_accessed=30_000_000, transcendentals=0),
        name="join_halves",
    )(skip, *acts, *pre_grads, up, up, down, down, inv_std, down_bias, scale, gain, whitened, tile, grad)


def kernel_grad_kernel(table_ref, tile_ref, *refs):
    strip_ref, grad_ref, out_ref, extended_ref, wide_ref, total_ref = refs
    assemble(table_ref, tile_ref, strip_ref, extended_ref)
    wide_ref[...] = grad_ref[...].astype(f32)
    total_ref[...] = jnp.zeros_like(total_ref)

    def rows(block, carry):
        base = block * row_block
        for w in range(side // 8):
            grads = [wide_ref[base + r, w * 8 : w * 8 + 8, :] for r in range(row_block)]
            for b in range(taps):
                start = own_column - rim + b + w * 8
                values = [extended_ref[base + r, start : start + 8, :] for r in range(row_block + taps - 1)]
                for a in range(taps):
                    terms = [values[r + a] * grads[r] for r in range(row_block)]
                    while len(terms) > 1:
                        terms = [terms[i] + terms[i + 1] for i in range(0, len(terms), 2)]
                    total_ref[a, b] += terms[0]
        return carry

    lax.fori_loop(0, side // row_block, rows, 0)
    for a in range(taps):
        out_ref[a] = jnp.sum(total_ref[a], axis=1)


def kernel_grad(table, tile, strips, conv_grad):
    channels = tile.shape[-1]
    block_spec = pl.BlockSpec((side, side, lanes), lambda i: (0, 0, i))
    return pl.pallas_call(
        kernel_grad_kernel,
        grid=(channels // lanes,),
        out_shape=jax.ShapeDtypeStruct((taps, taps, channels), f32),
        in_specs=[pl.BlockSpec(memory_space=pltpu.SMEM), block_spec, strip_spec(strips), block_spec],
        out_specs=pl.BlockSpec((taps, taps, lanes), lambda i: (0, 0, i)),
        scratch_shapes=[
            pltpu.VMEM((side + 2 * rim, wide, lanes), f32),
            pltpu.VMEM((side, side, lanes), f32),
            pltpu.VMEM((taps, taps, 8, lanes), f32),
        ],
        compiler_params=pltpu.CompilerParams(vmem_limit_bytes=small_limit),
        cost_estimate=pl.CostEstimate(flops=14_000_000_000, bytes_accessed=5_000_000, transcendentals=0),
        name="kernel_grad",
    )(table, tile, strips, conv_grad)


def back_kernel(table_ref, tile_ref, *refs):
    strip_ref, weight_ref, grad_ref = refs[:3]
    out_ref, extended_ref, spread_ref, total_ref = refs[-4:]
    assemble(table_ref, tile_ref, strip_ref, extended_ref)
    spread_weights(weight_ref, spread_ref, True)

    def store(row, column, value):
        total_ref[row, column : column + 8, :] = value

    depthwise(extended_ref, spread_ref, store)
    out_ref[...] = (grad_ref[...].astype(f32) + total_ref[...]).astype(bf16)


def back_conv(table, tile, strips, weight, grad, part, parts, done=None):
    channels = tile.shape[-1]
    steps = channels // lanes // parts
    first = part * steps
    block_spec = pl.BlockSpec((side, side, lanes), lambda i: (0, 0, first + i))
    earlier = [] if done is None else [done]
    return pl.pallas_call(
        back_kernel,
        grid=(steps,),
        out_shape=jax.ShapeDtypeStruct(tile.shape, bf16),
        in_specs=[
            pl.BlockSpec(memory_space=pltpu.SMEM),
            block_spec,
            strip_spec(strips, first),
            pl.BlockSpec((1, taps, taps, lanes), lambda i: (0, 0, 0, first + i)),
            block_spec,
            *[pl.BlockSpec(memory_space=pl.ANY) for _ in earlier],
        ],
        out_specs=block_spec,
        scratch_shapes=[
            pltpu.VMEM((side + 2 * rim, wide, lanes), f32),
            pltpu.VMEM((taps, taps, 8, lanes), f32),
            pltpu.VMEM((side, side, lanes), f32),
        ],
        input_output_aliases={5: 0} if earlier else {},
        compiler_params=pltpu.CompilerParams(vmem_limit_bytes=small_limit),
        cost_estimate=pl.CostEstimate(
            flops=14_000_000_000 // parts, bytes_accessed=5_000_000 // parts, transcendentals=0
        ),
        name="back_conv",
    )(table, tile, strips, weight, grad, *earlier)


def pick(value, positions):
    for axis, index in positions:
        value = lax.dynamic_index_in_dim(value, index, axis, keepdims=False)
    return value


def fold(parts, dtype):
    wide_parts = [part.astype(f32) for part in parts]
    while len(wide_parts) > 1:
        wide_parts = [wide_parts[i] + wide_parts[i + 1] for i in range(0, len(wide_parts), 2)]
    return wide_parts[0].astype(dtype)


def reduce_axis(take, distance, dtype):
    kept = take(0)
    arrived = [swap(take(k), k * distance) for k in (1, 2, 3)]
    return fold([kept, *arrived], dtype)


def place():
    slide, tile = lax.axis_index("slide"), lax.axis_index("tile")
    return slide // 4, (slide // 2) % 2, tile // 4, tile % 4


def x_parts(value):
    x = place()[3]
    return [pick(value, [(value.ndim - 3, x ^ k)]) for k in range(4)]


def y_parts(value):
    _, y_hi, y_lo, _ = place()
    return [pick(value, [(1, y_lo ^ (k % 2)), (0, y_hi ^ (k // 2))]) for k in range(4)]


def z_parts(value):
    z = place()[0]
    return [pick(value, [(0, z ^ k)]) for k in range(4)]


x_distances = (1, 2, 3)
y_distances = (4, 16, 20)
z_distances = (32, 64, 96)


def gather_sum(parts, distances, dtype, ready):
    arrived = [swap(part, d) for part, d in zip(parts[1:], distances)]
    return fold(gate([parts[0], *arrived], ready), dtype)


def gate(values, ready):
    return list(lax.optimization_barrier((*values, ready)))[: len(values)]


def after(value, *others):
    return lax.optimization_barrier((value, *others))[0]


def trade(value, distance, ready):
    value, arrived = gate([value, swap(value, distance)], ready)
    return value + arrived


def ride(parts, small):
    width = parts[0].shape[-1]
    extra = small.astype(bf16).reshape(-1, width)
    sent = [jnp.concatenate([part.reshape(-1, width), extra], 0) for part in parts[1:]]
    return sent, lax.reduce_precision(small, 8, 7)


def land(sent, small, parts, distances, dtype, ready):
    arrived = [swap(value, d) for value, d in zip(sent, distances)]
    size = parts[0].size // parts[0].shape[-1]
    mine, small, *arrived = gate([parts[0], small, *arrived], ready)
    total = fold([mine, *[value[:size].reshape(mine.shape) for value in arrived]], dtype)
    return total, fold([small, *[value[size:].reshape(small.shape) for value in arrived]], f32)


def on_device(
    features,
    cotangent,
    neighbours,
    skip_flags,
    dw_weight,
    ln_gain,
    ln_bias,
    up_weight,
    up_bias,
    down_weight,
    down_bias,
    layer_scale,
):
    channels = features.shape[-1]
    hidden = up_weight.shape[1]
    tile = features[0, 0]
    grad = cotangent[0, 0]
    flat = (side * side, channels)
    packed = pack_strips(neighbours, tile)
    strips = lax.all_to_all(packed, "tile", 0, 0)
    inner = conv_inner(after(tile, packed), dw_weight)
    strips = after(strips, inner)
    whitened, inv_std, normed = conv_norm(neighbours, inner, strips, dw_weight, ln_gain, ln_bias)
    flat_grad = grad.reshape(flat)
    bias_order = jnp.swapaxes(up_bias.reshape(4, 2, -1), 0, 1).reshape(4, 1, -1)
    mlp_in = (flat_grad, up_weight[0], bias_order, down_weight[0], layer_scale)
    act_low, pre_low, mine_low, theirs_low, bias_low = hidden_half(0, skip_flags, normed, *mlp_in)
    received_low = swap(theirs_low, 8)
    act_high, pre_high, mine_high, theirs_high, bias_high = hidden_half(1, skip_flags, after(normed, theirs_low), *mlp_in)
    rows = mine_low.shape[2] // 8
    width = mine_low.shape[3]
    grid = (4, 2, 4, rows, width)
    received_high = swap(theirs_high, 8)
    low_x = x_parts(fold(gate([mine_low, received_low], act_high), bf16).reshape(grid))
    high_z = z_parts(fold(gate([mine_high, received_high], tuple(low_x)), bf16).reshape(grid))
    got_high = [swap(high_z[1], 32), swap(high_z[3], 96)]
    out, conv_grad, channel_sums = join(
        skip_flags, (after(act_low, *low_x, *high_z), act_high), (pre_low, pre_high), up_weight[0], down_weight[0],
        inv_std, down_bias, layer_scale, ln_gain, whitened, tile.reshape(flat), flat_grad,
    )
    got_far = swap(after(high_z[2], conv_grad), 64)
    conv_grad = conv_grad.reshape(tile.shape)
    packed = pack_strips(neighbours, conv_grad)
    grad_strips = lax.all_to_all(packed, "tile", 0, 0)
    first, second, third = gate([high_z[0], *got_high], packed)
    near = first.astype(f32) + second.astype(f32) + third.astype(f32)
    low_z = z_parts(gather_sum(low_x, x_distances, bf16, packed))
    kernel_sums = kernel_grad(neighbours, tile, strips, after(conv_grad, near, *low_z))
    small = jnp.concatenate(
        [
            kernel_sums.reshape(taps * taps, channels),
            channel_sums,
            jnp.stack([bias_low.reshape(4, -1), bias_high.reshape(4, -1)], 1).reshape(-1, channels),
        ],
        0,
    )
    count = small.shape[0]
    small = jnp.pad(small, ((0, -count % 16), (0, 0)))
    done_low = gather_sum(low_z, z_distances, bf16, kernel_sums)
    high_x = x_parts(fold(gate([near, got_far], done_low), bf16))
    back = functools.partial(back_conv, neighbours)
    grad_strips = after(grad_strips, small)
    wide_x, small = ride(high_x, small)
    input_grad = back(after(conv_grad, *wide_x), grad_strips, dw_weight, grad, 0, 3)
    done_high, small = land(wide_x, small, high_x, x_distances, bf16, input_grad)
    last = y_parts(jnp.concatenate([done_low, done_high], 0).reshape(2, 2, rows, width))
    wide_y, small = ride(last, small)
    input_grad = back(after(conv_grad, *wide_y), grad_strips, dw_weight, grad, 1, 3, input_grad)
    weight_rows, small = land(wide_y, small, last, y_distances, f32, input_grad)
    sent_small = small.astype(bf16)
    got_small = [swap(sent_small, d) for d in z_distances]
    input_grad = back(after(conv_grad, sent_small), grad_strips, dw_weight, grad, 2, 3, input_grad)
    small = fold(gate([lax.reduce_precision(small, 8, 7), *got_small], input_grad), f32)
    small = trade(small, 8, small)[:count]
    split = taps * taps
    return (
        out.reshape(features.shape),
        input_grad[None, None],
        weight_rows[None],
        small[:split].reshape(1, taps, taps, channels),
        small[split : split + 4][None],
        small[split + 4 :].reshape(1, hidden),
    )


def solution(mesh):
    return jax.shard_map(
        on_device,
        mesh=mesh,
        in_specs=(
            P("slide", "tile", None, None, None),
            P("slide", "tile", None, None, None),
            P("slide", None, None),
            P(None, "slide"),
            P(),
            P(),
            P(),
            P(),
            P(),
            P(),
            P(),
            P(),
        ),
        out_specs=(
            P("slide", "tile", None, None, None),
            P("slide", "tile", None, None, None),
            P(None, ("slide", "tile"), None),
            P(),
            P(),
            P(),
        ),
        check_vma=False,
    )
```

```python
import functools

import jax
import jax.numpy as jnp
from jax import lax
from jax.experimental import pallas as pl
from jax.experimental.pallas import tpu as pltpu
from jax.sharding import PartitionSpec as P

ln_eps = 1e-06
root_half = 0.7071067811865476
inv_root_two_pi = 0.3989422804014327
f32 = jnp.float32
bf16 = jnp.bfloat16
both_axes = ("slide", "tile")
lanes = 128
side = 32
rim = 3
taps = 7
row_block = 16
own_column = 8
wide = 48
vmem_limit = 58 * 1024 * 1024
middle_limit = vmem_limit
small_limit = vmem_limit


def swap(value, distance):
    pairs = [(d, d ^ distance) for d in range(lax.axis_size(both_axes))]
    return lax.ppermute(value, both_axes, pairs)


def pack_kernel(table_ref, tile_ref, out_ref, column_ref, edge_ref):
    me = lax.axis_index("tile")
    tiles = out_ref.shape[0]
    channels = tile_ref.shape[-1]
    for block in range(channels // lanes):
        here = pl.ds(block * lanes, lanes)
        for which, start, first in ((0, 0, 0), (1, 16, 13)):
            column_ref[...] = tile_ref[:, start : start + 16, here].astype(f32).reshape(16 * side, lanes)
            for c in range(rim):
                edge_ref[which, c, :, here] = column_ref[pl.ds(first + c, side, stride=16), :].astype(bf16)
    sources = (
        lambda: tile_ref[0:rim],
        lambda: tile_ref[side - rim : side],
        lambda: edge_ref[0],
        lambda: edge_ref[1],
    )
    for direction, source in enumerate((0, 1, 2, 3, 0, 0, 1, 1)):
        other = table_ref[0, me, direction]

        @pl.when(other < tiles)
        def _():
            out_ref[other] = sources[source]()


def pack_strips(table, tile):
    tiles = table.shape[1]
    channels = tile.shape[-1]
    return pl.pallas_call(
        pack_kernel,
        out_shape=jax.ShapeDtypeStruct((tiles, rim, side, channels), bf16),
        in_specs=[pl.BlockSpec(memory_space=pltpu.SMEM), pl.BlockSpec(memory_space=pltpu.VMEM)],
        out_specs=pl.BlockSpec(memory_space=pltpu.VMEM),
        scratch_shapes=[
            pltpu.VMEM((16 * side, lanes), f32),
            pltpu.VMEM((2, rim, side, channels), bf16),
        ],
        compiler_params=pltpu.CompilerParams(vmem_limit_bytes=small_limit),
        name="pack_strips",
    )(table, tile)


def assemble(table_ref, tile_ref, strip_ref, extended_ref):
    me = lax.axis_index("tile")
    tiles = strip_ref.shape[0]
    extended_ref[rim : rim + side, own_column : own_column + side, :] = tile_ref[...].astype(f32)

    def strip(direction):
        other = table_ref[0, me, direction]
        values = strip_ref[jnp.minimum(other, tiles - 1)].astype(f32)
        return jnp.where(other < tiles, values, jnp.zeros_like(values))

    last = rim + side
    right = own_column + side
    extended_ref[0:rim, own_column:right, :] = strip(0)
    extended_ref[last : last + rim, own_column:right, :] = strip(1)
    west = strip(2)
    east = strip(3)
    for c in range(rim):
        extended_ref[rim:last, own_column - rim + c, :] = west[c]
        extended_ref[rim:last, right + c, :] = east[c]
    extended_ref[0:rim, 0:8, :] = strip(4)[:, side - 8 :]
    extended_ref[0:rim, right : right + 8, :] = strip(5)[:, :8]
    extended_ref[last : last + rim, 0:8, :] = strip(6)[:, side - 8 :]
    extended_ref[last : last + rim, right : right + 8, :] = strip(7)[:, :8]


def spread_weights(weight_ref, spread_ref, flipped):
    for a in range(taps):
        rows = weight_ref[0, taps - 1 - a if flipped else a]
        for b in range(taps):
            at = taps - 1 - b if flipped else b
            spread_ref[b, a] = jnp.broadcast_to(rows[at : at + 1], (8, lanes))


def depthwise(extended_ref, spread_ref, store):
    def rows(block, carry):
        base = block * row_block
        for w in range(side // 8):
            totals = [None] * row_block
            for b in range(taps):
                start = own_column - rim + b + w * 8
                values = [extended_ref[base + r, start : start + 8, :] for r in range(row_block + taps - 1)]
                for a in range(taps):
                    factor = spread_ref[b, a]
                    for r in range(row_block):
                        term = values[r + a] * factor
                        totals[r] = term if totals[r] is None else totals[r] + term
            for r in range(row_block):
                store(base + r, w * 8, totals[r])
        return carry

    lax.fori_loop(0, side // row_block, rows, 0)


def inner_kernel(tile_ref, weight_ref, out_ref, extended_ref, spread_ref):
    @pl.when(pl.program_id(0) == 0)
    def _():
        extended_ref[...] = jnp.zeros_like(extended_ref)

    extended_ref[rim : rim + side, own_column : own_column + side, :] = tile_ref[...].astype(f32)
    spread_weights(weight_ref, spread_ref, False)

    def store(row, column, value):
        out_ref[0, row, column : column + 8, :] = value

    depthwise(extended_ref, spread_ref, store)


def conv_inner(tile, weight):
    channels = tile.shape[-1]
    blocks = channels // lanes
    return pl.pallas_call(
        inner_kernel,
        grid=(blocks,),
        out_shape=jax.ShapeDtypeStruct((blocks, side, side, lanes), f32),
        in_specs=[
            pl.BlockSpec((side, side, lanes), lambda i: (0, 0, i)),
            pl.BlockSpec((1, taps, taps, lanes), lambda i: (0, 0, 0, i)),
        ],
        out_specs=pl.BlockSpec((1, side, side, lanes), lambda i: (i, 0, 0, 0)),
        scratch_shapes=[
            pltpu.VMEM((side + 2 * rim, wide, lanes), f32),
            pltpu.VMEM((taps, taps, 8, lanes), f32),
        ],
        compiler_params=pltpu.CompilerParams(vmem_limit_bytes=small_limit),
        cost_estimate=pl.CostEstimate(flops=14_000_000_000, bytes_accessed=5_000_000, transcendentals=0),
        name="conv_inner",
    )(tile, weight)


def add_rim(table_ref, strip_ref, spread_ref, rows_ref, edge_ref, conv_ref, block):
    me = lax.axis_index("tile")
    tiles = strip_ref.shape[0]

    def strip(direction):
        other = table_ref[0, me, direction]
        values = strip_ref[jnp.minimum(other, tiles - 1)].astype(f32)
        return jnp.where(other < tiles, values, jnp.zeros_like(values))

    right = own_column + side
    for at, (middle, left, end) in enumerate(((0, 4, 5), (1, 6, 7))):
        rows_ref[at, :, own_column:right, :] = strip(middle)
        rows_ref[at, :, 0:8, :] = strip(left)[:, side - 8 :]
        rows_ref[at, :, right : right + 8, :] = strip(end)[:, :8]
    west, east = strip(2), strip(3)
    for c in range(rim):
        edge_ref[0, rim : rim + side, own_column - rim + c, :] = west[c]
        edge_ref[1, rim : rim + side, 8 + c, :] = east[c]

    for w in range(side // 8):
        for at, row, terms in (
            (0, 0, ((0, 0), (1, 1), (2, 2))),
            (0, 1, ((1, 0), (2, 1))),
            (0, 2, ((2, 0),)),
            (1, side - 1, ((0, 4), (1, 5), (2, 6))),
            (1, side - 2, ((0, 5), (1, 6))),
            (1, side - 3, ((0, 6),)),
        ):
            total = conv_ref[block, row, w * 8 : w * 8 + 8, :]
            for b in range(taps):
                start = own_column - rim + b + w * 8
                for source, a in terms:
                    total = total + rows_ref[at, source, start : start + 8, :] * spread_ref[b, a]
            conv_ref[block, row, w * 8 : w * 8 + 8, :] = total

    def columns(part, carry):
        base = part * row_block
        for which, w, picks in ((0, 0, ((0, 5), (1, 6), (2, 7))), (1, side // 8 - 1, ((4, 1), (5, 2), (6, 3)))):
            here = slice(w * 8, w * 8 + 8)
            totals = [conv_ref[block, base + r, here, :] for r in range(row_block)]
            for b, start in picks:
                values = [edge_ref[which, base + r, start : start + 8, :] for r in range(row_block + taps - 1)]
                for a in range(taps):
                    factor = spread_ref[b, a]
                    for r in range(row_block):
                        totals[r] = totals[r] + values[r + a] * factor
            for r in range(row_block):
                conv_ref[block, base + r, here, :] = totals[r]
        return carry

    lax.fori_loop(0, side // row_block, columns, 0)


def norm_kernel(
    table_ref, part_ref, strip_ref, weight_ref, gain_ref, shift_ref,
    whitened_ref, inv_ref, normed_ref, spread_ref, rows_ref, edge_ref, conv_ref,
):
    block = pl.program_id(0)
    blocks = whitened_ref.shape[1] // lanes

    @pl.when(block == 0)
    def _():
        edge_ref[...] = jnp.zeros_like(edge_ref)

    spread_weights(weight_ref, spread_ref, False)
    conv_ref[block] = part_ref[0]
    add_rim(table_ref, strip_ref, spread_ref, rows_ref, edge_ref, conv_ref, block)

    @pl.when(block == blocks - 1)
    def _():
        def norm(row, carry):
            parts = [conv_ref[j, row] for j in range(blocks)]
            count = blocks * lanes
            average = jnp.sum(sum(parts), axis=-1, keepdims=True) / count
            centred = [part - average for part in parts]
            spread = jnp.sum(sum(part * part for part in centred), axis=-1, keepdims=True) / count
            inv_std = lax.rsqrt(spread + ln_eps)
            here = pl.ds(pl.multiple_of(row * side, side), side)
            inv_ref[here, :] = inv_std
            for j in range(blocks):
                at = pl.ds(j * lanes, lanes)
                whitened = centred[j] * inv_std
                whitened_ref[here, at] = whitened
                normed_ref[here, at] = (whitened * gain_ref[:, at] + shift_ref[:, at]).astype(bf16)
            return carry

        lax.fori_loop(0, side, norm, 0, unroll=4)


def strip_spec(strips, first=0):
    return pl.BlockSpec((*strips.shape[:3], lanes), lambda i: (0, 0, 0, first + i))


def conv_norm(table, part, strips, weight, gain, shift):
    blocks = part.shape[0]
    channels = blocks * lanes
    pixels = side * side
    whole = lambda i: (0, 0)
    return pl.pallas_call(
        norm_kernel,
        grid=(blocks,),
        out_shape=[
            jax.ShapeDtypeStruct((pixels, channels), f32),
            jax.ShapeDtypeStruct((pixels, 1), f32),
            jax.ShapeDtypeStruct((pixels, channels), bf16),
        ],
        in_specs=[
            pl.BlockSpec(memory_space=pltpu.SMEM),
            pl.BlockSpec((1, side, side, lanes), lambda i: (i, 0, 0, 0)),
            strip_spec(strips),
            pl.BlockSpec((1, taps, taps, lanes), lambda i: (0, 0, 0, i)),
            pl.BlockSpec((1, channels), whole),
            pl.BlockSpec((1, channels), whole),
        ],
        out_specs=[full(pixels, channels), full(pixels, 1), full(pixels, channels)],
        scratch_shapes=[
            pltpu.VMEM((taps, taps, 8, lanes), f32),
            pltpu.VMEM((2, rim, wide, lanes), f32),
            pltpu.VMEM((2, side + 2 * rim, 16, lanes), f32),
            pltpu.VMEM((blocks, side, side, lanes), f32),
        ],
        compiler_params=pltpu.CompilerParams(vmem_limit_bytes=middle_limit),
        cost_estimate=pl.CostEstimate(flops=7_000_000_000, bytes_accessed=10_000_000, transcendentals=0),
        name="conv_norm",
    )(table, part, strips, weight, gain, shift)


dot = functools.partial(lax.dot_general, preferred_element_type=f32)
by_rows = (((1,), (1,)), ((), ()))
plain = (((1,), (0,)), ((), ()))
by_pixels = (((0,), (0,)), ((), ()))


def join_blocks(up_first_ref, up_second_ref, down_first_ref, down_second_ref, up_ref, down_ref):
    block = up_first_ref.shape[0]
    up_ref[:block] = up_first_ref[...]
    up_ref[block:] = up_second_ref[...]
    down_ref[:, :block] = down_first_ref[...]
    down_ref[:, block:] = down_second_ref[...]


def hidden_kernel(
    skip_ref, normed_ref, grad_ref, up_first_ref, up_second_ref, up_bias_ref, down_first_ref, down_second_ref,
    scale_ref,
    act_ref, pre_grad_ref, mine_ref, theirs_ref, bias_ref,
    branch_grad_ref, pair_ref, up_ref, down_ref,
):
    step = pl.program_id(0)
    pixels, channels = normed_ref.shape
    keep = (1 - skip_ref[0, 0]).astype(f32)
    tile_rows = 256
    join_blocks(up_first_ref, up_second_ref, down_first_ref, down_second_ref, up_ref, down_ref)

    @pl.when(step == 0)
    def _():
        branch_grad_ref[...] = (keep * scale_ref[...] * grad_ref[...].astype(f32)).astype(bf16)

    def rows_of(m):
        return pl.ds(m * tile_rows, tile_rows)

    def lift(m):
        return dot(normed_ref[rows_of(m), :], up_ref[...], by_rows) + up_bias_ref[0]

    bias_sum = jnp.zeros((1, up_ref.shape[0]), f32)
    count = pixels // tile_rows
    following = lift(0)
    for m in range(count):
        rows = rows_of(m)
        pre = following
        act_grad = dot(branch_grad_ref[rows, :], down_ref[...], plain)
        if m + 1 < count:
            following = lift(m + 1)
        cdf = 0.5 * (1.0 + lax.erf(pre * root_half))
        slope = cdf + pre * inv_root_two_pi * jnp.exp(-0.5 * pre * pre)
        act_ref[rows, :] = (pre * cdf).astype(bf16)
        pre_grad = (act_grad * slope).astype(bf16)
        pre_grad_ref[rows, :] = pre_grad
        bias_sum = bias_sum + jnp.sum(pre_grad.astype(f32), axis=0, keepdims=True)
    bias_ref[0] = bias_sum
    quarter = pair_ref.shape[1]
    left = dot(pre_grad_ref[...], normed_ref[...], by_pixels).astype(bf16)
    for q in range(4):
        pair_ref[q, :, :channels] = left[q * quarter : (q + 1) * quarter]
    right = dot(act_ref[...], branch_grad_ref[...], by_pixels).astype(bf16)
    for q in range(4):
        pair_ref[q, :, channels:] = right[q * quarter : (q + 1) * quarter]
    core = lax.axis_index("slide") % 2
    for high in range(2):
        mine_ref[0, high] = pair_ref[2 * high + core]
        theirs_ref[0, high] = pair_ref[2 * high + 1 - core]


once = pl.Buffered(1)
anywhere = pl.BlockSpec(memory_space=pl.ANY)
in_scalars = pl.BlockSpec(memory_space=pltpu.SMEM)


def full(*shape):
    return pl.BlockSpec(shape, lambda i: (0, 0), pipeline_mode=once)


def hidden_half(half, skip, normed, grad, up, up_bias, down, scale):
    pixels, channels = normed.shape
    hidden = up.shape[0]
    steps = 2
    chunk = hidden // 4
    quarter = chunk // 4
    block = chunk // 2
    part = jax.ShapeDtypeStruct((steps, 2, quarter, 2 * channels), bf16)
    part_spec = pl.BlockSpec((1, 2, quarter, 2 * channels), lambda i: (i, 0, 0, 0))
    wide_shape = jax.ShapeDtypeStruct((pixels, steps * chunk), bf16)
    wide_spec = pl.BlockSpec((pixels, chunk), lambda i: (0, i))
    return pl.pallas_call(
        hidden_kernel,
        grid=(steps,),
        out_shape=[wide_shape, wide_shape, part, part, jax.ShapeDtypeStruct((steps, 1, chunk), f32)],
        in_specs=[
            in_scalars,
            full(pixels, channels),
            full(pixels, channels),
            pl.BlockSpec((block, channels), lambda i: (4 * i + half, 0)),
            pl.BlockSpec((block, channels), lambda i: (4 * i + 2 + half, 0)),
            pl.BlockSpec((1, 1, chunk), lambda i: (2 * half + i, 0, 0)),
            pl.BlockSpec((channels, block), lambda i: (0, 4 * i + half)),
            pl.BlockSpec((channels, block), lambda i: (0, 4 * i + 2 + half)),
            full(1, channels),
        ],
        out_specs=[wide_spec, wide_spec, part_spec, part_spec, pl.BlockSpec((1, 1, chunk), lambda i: (i, 0, 0))],
        scratch_shapes=[
            pltpu.VMEM((pixels, channels), bf16),
            pltpu.VMEM((4, quarter, 2 * channels), bf16),
            pltpu.VMEM((chunk, channels), bf16),
            pltpu.VMEM((channels, chunk), bf16),
        ],
        compiler_params=pltpu.CompilerParams(vmem_limit_bytes=vmem_limit),
        cost_estimate=pl.CostEstimate(flops=14_000_000_000, bytes_accessed=20_000_000, transcendentals=0),
        name="hidden_half",
    )(skip, normed, grad, up, up, up_bias, down, down, scale)


def join_kernel(
    skip_ref, act_low_ref, act_high_ref, pre_low_ref, pre_high_ref,
    up_first_ref, up_second_ref, down_first_ref, down_second_ref, inv_ref, down_bias_ref, scale_ref, gain_ref, whitened_hbm_ref, tile_hbm_ref, grad_hbm_ref,
    out_ref, conv_grad_ref, channel_ref,
    branch_ref, normed_grad_ref, whitened_ref, tile_ref, grad_ref, arrived, up_ref, down_ref,
):
    step = pl.program_id(0)
    steps = pl.num_programs(0)
    pixels, channels = out_ref.shape
    pairs = ((whitened_hbm_ref, whitened_ref), (tile_hbm_ref, tile_ref), (grad_hbm_ref, grad_ref))
    copies = [pltpu.make_async_copy(*pair, arrived.at[at]) for at, pair in enumerate(pairs)]
    join_blocks(up_first_ref, up_second_ref, down_first_ref, down_second_ref, up_ref, down_ref)

    @pl.when(step == 0)
    def _():
        for copy in copies:
            copy.start()
        branch_ref[...] = dot(act_low_ref[...], down_ref[...], by_rows)
        normed_grad_ref[...] = dot(pre_low_ref[...], up_ref[...], plain)

    @pl.when(step == 1)
    def _():
        branch_ref[...] += dot(act_low_ref[...], down_ref[...], by_rows)
        normed_grad_ref[...] += dot(pre_low_ref[...], up_ref[...], plain)

    @pl.when(step >= 2)
    def _():
        branch_ref[...] += dot(act_high_ref[...], down_ref[...], by_rows)
        normed_grad_ref[...] += dot(pre_high_ref[...], up_ref[...], plain)

    @pl.when(step == steps - 1)
    def _():
        rows_each = 64
        keep = (1 - skip_ref[0, 0]).astype(f32)
        factor = keep * scale_ref[...]
        for copy in copies:
            copy.wait()

        def finish(m, sums):
            rows = pl.ds(pl.multiple_of(m * rows_each, rows_each), rows_each)
            grad = grad_ref[rows, :].astype(f32)
            branch = branch_ref[rows, :] + down_bias_ref[...]
            out_ref[rows, :] = (tile_ref[rows, :].astype(f32) + factor * branch).astype(bf16)
            whitened = whitened_ref[rows, :]
            normed_grad = normed_grad_ref[rows, :]
            scaled = normed_grad * gain_ref[...]
            product = normed_grad * whitened
            mean_one = jnp.sum(scaled, axis=-1, keepdims=True) / channels
            mean_two = jnp.sum(scaled * whitened, axis=-1, keepdims=True) / channels
            conv_grad = inv_ref[rows, :] * (scaled - mean_one - whitened * mean_two)
            conv_grad_ref[rows, :] = conv_grad.astype(bf16)
            branch_grad = (factor * grad).astype(bf16).astype(f32)
            terms = (product, normed_grad, branch_grad, grad * keep * branch)
            return tuple(
                total + jnp.sum(term.reshape(rows_each // 8, 8, channels), axis=0)
                for total, term in zip(sums, terms)
            )

        zero = jnp.zeros((8, channels), f32)
        sums = lax.fori_loop(0, pixels // rows_each, finish, (zero,) * 4, unroll=2)
        for at in range(4):
            channel_ref[at : at + 1, :] = jnp.sum(sums[at], axis=0, keepdims=True)


def join(skip, acts, pre_grads, up, down, inv_std, down_bias, scale, gain, whitened, tile, grad):
    pixels, channels = grad.shape
    chunk = acts[0].shape[1] // 2
    block = chunk // 2
    at_first = lambda i: 4 * (i % 2) + i // 2
    low_spec = pl.BlockSpec((pixels, chunk), lambda i: (0, jnp.minimum(i, 1)))
    high_spec = pl.BlockSpec((pixels, chunk), lambda i: (0, jnp.maximum(i - 2, 0)))
    pixel = jax.ShapeDtypeStruct((pixels, channels), bf16)
    return pl.pallas_call(
        join_kernel,
        grid=(4,),
        out_shape=[pixel, pixel, jax.ShapeDtypeStruct((4, channels), f32)],
        in_specs=[
            in_scalars,
            low_spec,
            high_spec,
            low_spec,
            high_spec,
            pl.BlockSpec((block, channels), lambda i: (at_first(i), 0)),
            pl.BlockSpec((block, channels), lambda i: (at_first(i) + 2, 0)),
            pl.BlockSpec((channels, block), lambda i: (0, at_first(i))),
            pl.BlockSpec((channels, block), lambda i: (0, at_first(i) + 2)),
            full(pixels, 1),
            full(1, channels),
            full(1, channels),
            full(1, channels),
            anywhere,
            anywhere,
            anywhere,
        ],
        out_specs=[full(pixels, channels), full(pixels, channels), full(4, channels)],
        scratch_shapes=[
            pltpu.VMEM((pixels, channels), f32),
            pltpu.VMEM((pixels, channels), f32),
            pltpu.VMEM((pixels, channels), f32),
            pltpu.VMEM((pixels, channels), bf16),
            pltpu.VMEM((pixels, channels), bf16),
            pltpu.SemaphoreType.DMA((3,)),
            pltpu.VMEM((chunk, channels), bf16),
            pltpu.VMEM((channels, chunk), bf16),
        ],
        compiler_params=pltpu.CompilerParams(vmem_limit_bytes=vmem_limit),
        cost_estimate=pl.CostEstimate(flops=14_000_000_000, bytes_accessed=30_000_000, transcendentals=0),
        name="join_halves",
    )(skip, *acts, *pre_grads, up, up, down, down, inv_std, down_bias, scale, gain, whitened, tile, grad)


def kernel_grad_kernel(table_ref, tile_ref, *refs):
    strip_ref, grad_ref, out_ref, extended_ref, wide_ref, total_ref = refs
    assemble(table_ref, tile_ref, strip_ref, extended_ref)
    wide_ref[...] = grad_ref[...].astype(f32)
    total_ref[...] = jnp.zeros_like(total_ref)

    def rows(block, carry):
        base = block * row_block
        for w in range(side // 8):
            grads = [wide_ref[base + r, w * 8 : w * 8 + 8, :] for r in range(row_block)]
            for b in range(taps):
                start = own_column - rim + b + w * 8
                values = [extended_ref[base + r, start : start + 8, :] for r in range(row_block + taps - 1)]
                for a in range(taps):
                    terms = [values[r + a] * grads[r] for r in range(row_block)]
                    while len(terms) > 1:
                        terms = [terms[i] + terms[i + 1] for i in range(0, len(terms), 2)]
                    total_ref[a, b] += terms[0]
        return carry

    lax.fori_loop(0, side // row_block, rows, 0)
    for a in range(taps):
        out_ref[a] = jnp.sum(total_ref[a], axis=1)


def kernel_grad(table, tile, strips, conv_grad):
    channels = tile.shape[-1]
    block_spec = pl.BlockSpec((side, side, lanes), lambda i: (0, 0, i))
    return pl.pallas_call(
        kernel_grad_kernel,
        grid=(channels // lanes,),
        out_shape=jax.ShapeDtypeStruct((taps, taps, channels), f32),
        in_specs=[pl.BlockSpec(memory_space=pltpu.SMEM), block_spec, strip_spec(strips), block_spec],
        out_specs=pl.BlockSpec((taps, taps, lanes), lambda i: (0, 0, i)),
        scratch_shapes=[
            pltpu.VMEM((side + 2 * rim, wide, lanes), f32),
            pltpu.VMEM((side, side, lanes), f32),
            pltpu.VMEM((taps, taps, 8, lanes), f32),
        ],
        compiler_params=pltpu.CompilerParams(vmem_limit_bytes=small_limit),
        cost_estimate=pl.CostEstimate(flops=14_000_000_000, bytes_accessed=5_000_000, transcendentals=0),
        name="kernel_grad",
    )(table, tile, strips, conv_grad)


def back_kernel(table_ref, tile_ref, *refs):
    strip_ref, weight_ref, grad_ref = refs[:3]
    out_ref, extended_ref, spread_ref, total_ref = refs[-4:]
    assemble(table_ref, tile_ref, strip_ref, extended_ref)
    spread_weights(weight_ref, spread_ref, True)

    def store(row, column, value):
        total_ref[row, column : column + 8, :] = value

    depthwise(extended_ref, spread_ref, store)
    out_ref[...] = (grad_ref[...].astype(f32) + total_ref[...]).astype(bf16)


def back_conv(table, tile, strips, weight, grad, part, parts, done=None):
    channels = tile.shape[-1]
    steps = channels // lanes // parts
    first = part * steps
    block_spec = pl.BlockSpec((side, side, lanes), lambda i: (0, 0, first + i))
    earlier = [] if done is None else [done]
    return pl.pallas_call(
        back_kernel,
        grid=(steps,),
        out_shape=jax.ShapeDtypeStruct(tile.shape, bf16),
        in_specs=[
            pl.BlockSpec(memory_space=pltpu.SMEM),
            block_spec,
            strip_spec(strips, first),
            pl.BlockSpec((1, taps, taps, lanes), lambda i: (0, 0, 0, first + i)),
            block_spec,
            *[pl.BlockSpec(memory_space=pl.ANY) for _ in earlier],
        ],
        out_specs=block_spec,
        scratch_shapes=[
            pltpu.VMEM((side + 2 * rim, wide, lanes), f32),
            pltpu.VMEM((taps, taps, 8, lanes), f32),
            pltpu.VMEM((side, side, lanes), f32),
        ],
        input_output_aliases={5: 0} if earlier else {},
        compiler_params=pltpu.CompilerParams(vmem_limit_bytes=small_limit),
        cost_estimate=pl.CostEstimate(
            flops=14_000_000_000 // parts, bytes_accessed=5_000_000 // parts, transcendentals=0
        ),
        name="back_conv",
    )(table, tile, strips, weight, grad, *earlier)


def pick(value, positions):
    for axis, index in positions:
        value = lax.dynamic_index_in_dim(value, index, axis, keepdims=False)
    return value


def fold(parts, dtype):
    wide_parts = [part.astype(f32) for part in parts]
    while len(wide_parts) > 1:
        wide_parts = [wide_parts[i] + wide_parts[i + 1] for i in range(0, len(wide_parts), 2)]
    return wide_parts[0].astype(dtype)


def reduce_axis(take, distance, dtype):
    kept = take(0)
    arrived = [swap(take(k), k * distance) for k in (1, 2, 3)]
    return fold([kept, *arrived], dtype)


def place():
    slide, tile = lax.axis_index("slide"), lax.axis_index("tile")
    return slide // 4, (slide // 2) % 2, tile // 4, tile % 4


def x_parts(value):
    x = place()[3]
    return [pick(value, [(value.ndim - 3, x ^ k)]) for k in range(4)]


def y_parts(value):
    _, y_hi, y_lo, _ = place()
    return [pick(value, [(1, y_lo ^ (k % 2)), (0, y_hi ^ (k // 2))]) for k in range(4)]


def z_parts(value):
    z = place()[0]
    return [pick(value, [(0, z ^ k)]) for k in range(4)]


x_distances = (1, 2, 3)
y_distances = (4, 16, 20)
z_distances = (32, 64, 96)


def gather_sum(parts, distances, dtype, ready):
    arrived = [swap(part, d) for part, d in zip(parts[1:], distances)]
    return fold(gate([parts[0], *arrived], ready), dtype)


def gate(values, ready):
    return list(lax.optimization_barrier((*values, ready)))[: len(values)]


def after(value, *others):
    return lax.optimization_barrier((value, *others))[0]


def trade(value, distance, ready):
    value, arrived = gate([value, swap(value, distance)], ready)
    return value + arrived


def ride(parts, small):
    width = parts[0].shape[-1]
    extra = small.astype(bf16).reshape(-1, width)
    sent = [jnp.concatenate([part.reshape(-1, width), extra], 0) for part in parts[1:]]
    return sent, lax.reduce_precision(small, 8, 7)


def land(sent, small, parts, distances, dtype, ready):
    arrived = [swap(value, d) for value, d in zip(sent, distances)]
    size = parts[0].size // parts[0].shape[-1]
    mine, small, *arrived = gate([parts[0], small, *arrived], ready)
    total = fold([mine, *[value[:size].reshape(mine.shape) for value in arrived]], dtype)
    return total, fold([small, *[value[size:].reshape(small.shape) for value in arrived]], f32)


def on_device(
    features,
    cotangent,
    neighbours,
    skip_flags,
    dw_weight,
    ln_gain,
    ln_bias,
    up_weight,
    up_bias,
    down_weight,
    down_bias,
    layer_scale,
):
    channels = features.shape[-1]
    hidden = up_weight.shape[1]
    tile = features[0, 0]
    grad = cotangent[0, 0]
    flat = (side * side, channels)
    packed = pack_strips(neighbours, tile)
    strips = lax.all_to_all(packed, "tile", 0, 0)
    inner = conv_inner(after(tile, packed), dw_weight)
    strips = after(strips, inner)
    whitened, inv_std, normed = conv_norm(neighbours, inner, strips, dw_weight, ln_gain, ln_bias)
    flat_grad = grad.reshape(flat)
    bias_order = jnp.swapaxes(up_bias.reshape(4, 2, -1), 0, 1).reshape(4, 1, -1)
    mlp_in = (flat_grad, up_weight[0], bias_order, down_weight[0], layer_scale)
    act_low, pre_low, mine_low, theirs_low, bias_low = hidden_half(0, skip_flags, normed, *mlp_in)
    received_low = swap(theirs_low, 8)
    act_high, pre_high, mine_high, theirs_high, bias_high = hidden_half(1, skip_flags, after(normed, theirs_low), *mlp_in)
    rows = mine_low.shape[2] // 8
    width = mine_low.shape[3]
    grid = (4, 2, 4, rows, width)
    received_high = swap(theirs_high, 8)
    low_x = x_parts(fold(gate([mine_low, received_low], act_high), bf16).reshape(grid))
    high_z = z_parts(fold(gate([mine_high, received_high], tuple(low_x)), bf16).reshape(grid))
    got_high = [swap(high_z[1], 32), swap(high_z[3], 96)]
    out, conv_grad, channel_sums = join(
        skip_flags, (after(act_low, *low_x, *high_z), act_high), (pre_low, pre_high), up_weight[0], down_weight[0],
        inv_std, down_bias, layer_scale, ln_gain, whitened, tile.reshape(flat), flat_grad,
    )
    got_far = swap(after(high_z[2], conv_grad), 64)
    conv_grad = conv_grad.reshape(tile.shape)
    packed = pack_strips(neighbours, conv_grad)
    grad_strips = lax.all_to_all(packed, "tile", 0, 0)
    first, second, third = gate([high_z[0], *got_high], packed)
    near = first.astype(f32) + second.astype(f32) + third.astype(f32)
    low_z = z_parts(gather_sum(low_x, x_distances, bf16, packed))
    kernel_sums = kernel_grad(neighbours, tile, strips, after(conv_grad, near, *low_z))
    small = jnp.concatenate(
        [
            kernel_sums.reshape(taps * taps, channels),
            channel_sums,
            jnp.stack([bias_low.reshape(4, -1), bias_high.reshape(4, -1)], 1).reshape(-1, channels),
        ],
        0,
    )
    count = small.shape[0]
    small = jnp.pad(small, ((0, -count % 16), (0, 0)))
    done_low = gather_sum(low_z, z_distances, bf16, kernel_sums)
    high_x = x_parts(fold(gate([near, got_far], done_low), bf16))
    back = functools.partial(back_conv, neighbours)
    grad_strips = after(grad_strips, small)
    small = trade(small, 8, tuple(high_x))
    wide_x, small = ride(high_x, small)
    input_grad = back(after(conv_grad, *wide_x), grad_strips, dw_weight, grad, 0, 3)
    done_high, small = land(wide_x, small, high_x, x_distances, bf16, input_grad)
    last = y_parts(jnp.concatenate([done_low, done_high], 0).reshape(2, 2, rows, width))
    wide_y, small = ride(last, small)
    input_grad = back(after(conv_grad, *wide_y), grad_strips, dw_weight, grad, 1, 3, input_grad)
    weight_rows, small = land(wide_y, small, last, y_distances, f32, input_grad)
    sent_small = small.astype(bf16)
    got_small = [swap(sent_small, d) for d in z_distances]
    input_grad = back(after(conv_grad, sent_small), grad_strips, dw_weight, grad, 2, 3, input_grad)
    small = fold(gate([lax.reduce_precision(small, 8, 7), *got_small], input_grad), f32)[:count]
    split = taps * taps
    return (
        out.reshape(features.shape),
        input_grad[None, None],
        weight_rows[None],
        small[:split].reshape(1, taps, taps, channels),
        small[split : split + 4][None],
        small[split + 4 :].reshape(1, hidden),
    )


def solution(mesh):
    return jax.shard_map(
        on_device,
        mesh=mesh,
        in_specs=(
            P("slide", "tile", None, None, None),
            P("slide", "tile", None, None, None),
            P("slide", None, None),
            P(None, "slide"),
            P(),
            P(),
            P(),
            P(),
            P(),
            P(),
            P(),
            P(),
        ),
        out_specs=(
            P("slide", "tile", None, None, None),
            P("slide", "tile", None, None, None),
            P(None, ("slide", "tile"), None),
            P(),
            P(),
            P(),
        ),
        check_vma=False,
    )
```
